256 devices in a mesh: ctx: 64 (over x, z, core), tp: 4 (over y).
Axes of the slice: x: 4, y: 4, z: 8, core: 2. Of those that a mesh axis runs over, the one named last changes fastest.
Arguments:
- query: bfloat16 [32768, 4096], P('ctx', 'tp'), may hold values from -6 to 6
- key_in: bfloat16 [32768, 4096], P('ctx', 'tp'), may hold values from -6 to 6
- value: bfloat16 [32768, 4096], P('ctx', 'tp'), may hold values from -6 to 6
- rates: float32 [256, 16], P('tp'), as said below
- residues: float32 [256, 16], P('tp'), as said below
- skip_gain: float32 [4096], P('tp'), may hold values from 0.5 to 1.5
- out_weight: bfloat16 [4096, 4096], P('tp'), may hold values from -0.09375 to 0.09375
Outputs:
- layer_out: bfloat16 [32768, 4096], P('ctx', 'tp')
The draws below stay inside these ranges and needn't reach their ends.
Inputs may be any that keep to these rules, and one draw needn't show every extreme that they name: `rates`: positive, at most 0.0625. `residues`: either sign.
All inputs are finite; a program needn't handle non-finite values.
Results may differ from the reference program's by a relative error of at most 0.0095.
Values may be sent and summed in bfloat16 or wider, within the bound.
A program may use at most 128 MiB of HBM per device.

```python
import jax
import jax.numpy as jnp
from jax import lax

D = 4096
GROUP = 16
MODES = 16
TOK_DEV = 512
GROUPS = 256
SEQ = 32768
N_CTX = 64


def mode_table(key, ceiling):
    first, second = jax.random.split(jax.random.fold_in(key, 11))
    floor_rate = 0.5 / SEQ
    spread_draw = jax.random.uniform(first, (GROUPS, MODES), jnp.float32)
    rate_values = jnp.exp(jnp.log(floor_rate) + spread_draw * (jnp.log(ceiling) - jnp.log(floor_rate)))
    weights_drawn = jax.random.normal(second, (GROUPS, MODES), jnp.float32) * jnp.sqrt(2.0 * rate_values / MODES)
    return (rate_values, weights_drawn)


def draw_rates(key, part):
    ceiling = 0.0625
    return mode_table(key, ceiling)[0]


def draw_residues(key, part):
    ceiling = 0.0625
    return mode_table(key, ceiling)[1]


def level_of(key, shape, pieces, smallest, top_value):
    level, own = 1.0, jax.random.fold_in(key, 6)
    for position, blocks in pieces:
        heights = jnp.exp(jax.random.uniform(jax.random.fold_in(own, position), (blocks,), jnp.float32, smallest / len(pieces), top_value / len(pieces)))
        level = level * jnp.repeat(heights, shape[position] // blocks).reshape([-1 if axis == position else 1 for axis in range(len(shape))])
    return level


def centred(stream_key, shape, spread, reach, shards=(), held_as=jnp.bfloat16):
    entries = spread * jax.random.normal(stream_key, shape, jnp.float32)
    if shards:
        entries = entries * level_of(stream_key, shape, shards, -0.22, 0.18)
    return jnp.clip(entries, -reach, reach).astype(held_as)


def setup_inputs(seed: int = 0) -> dict:
    streams_of = jax.random.split(jax.random.key(seed), 8)
    return {
        "query": centred(streams_of[0], (SEQ, D), 1.0, 6.0, ((0, 64), (1, 4))),
        "key_in": centred(streams_of[1], (SEQ, D), 1.0, 6.0, ((0, 64), (1, 4))),
        "value": centred(streams_of[2], (SEQ, D), 1.0, 6.0, ((0, 64), (1, 4))),
        "rates": draw_rates(jax.random.fold_in(streams_of[7], 71), 0),
        "residues": draw_residues(jax.random.fold_in(streams_of[7], 71), 0),
        "skip_gain": jnp.clip(0.5 + 1.0 * jax.random.uniform(streams_of[5], (D,), jnp.float32) ** level_of(streams_of[5], (D,), ((0, 4),), -0.2, 0.2), 0.5, 1.5),
        "out_weight": centred(streams_of[6], (D, D), D ** -0.5, 0.09375, ((0, 4),)),
    }


def reference(query, key_in, value, rates, residues, skip_gain, out_weight):
    product_bf = (key_in.astype(jnp.float32) * value.astype(jnp.float32)).astype(jnp.bfloat16)
    signal = product_bf.astype(jnp.float32)
    groups_all = D // GROUP
    block_rows = TOK_DEV
    positions = jnp.arange(block_rows, dtype=jnp.float32)
    filter_local = jnp.sum(residues[:, :, None] * jnp.exp(-rates[:, :, None] * positions[None, None, :]), axis=1)
    lag_index = (jnp.arange(block_rows, dtype=jnp.int32)[:, None] - jnp.arange(block_rows, dtype=jnp.int32)[None, :]).astype(jnp.int32)
    toeplitz = jnp.where(lag_index[None] >= 0, jnp.take(filter_local, jnp.clip(lag_index, 0, block_rows - 1), axis=1), jnp.float32(0.0))
    rate_cols = jnp.repeat(rates, GROUP, axis=0).T
    residue_cols = jnp.repeat(residues, GROUP, axis=0).T
    decay_in = jnp.exp(-rate_cols[:, :, None] * (block_rows - 1.0 - positions)[None, None, :])
    decay_out = residue_cols[:, :, None] * jnp.exp(-rate_cols[:, :, None] * (positions + 1.0)[None, None, :])
    block_decay = jnp.exp(-rate_cols * block_rows)
    blocks_in = signal.reshape(N_CTX, block_rows, D)

    def advance(state, block):
        channel_first = block.T
        local = jnp.einsum("gts,gcs->gct", toeplitz, channel_first.reshape(groups_all, GROUP, block_rows), precision=lax.Precision.HIGHEST).reshape(D, block_rows)
        past = jnp.einsum("mct,mc->ct", decay_out, state, precision=lax.Precision.HIGHEST)
        summary = jnp.einsum("mcs,cs->mc", decay_in, channel_first, precision=lax.Precision.HIGHEST)
        return block_decay * state + summary, (local + past).T

    _, conv_blocks = lax.scan(advance, jnp.zeros((MODES, D), jnp.float32), blocks_in)
    conv = conv_blocks.reshape(signal.shape)
    mixed = (query.astype(jnp.float32) * (conv + skip_gain[None, :] * signal)).astype(jnp.bfloat16)
    return jnp.dot(mixed, out_weight, preferred_element_type=jnp.float32).astype(jnp.bfloat16)
```

```python
import functools

import jax
import jax.numpy as jnp
from jax import lax
from jax.experimental import pallas as pl
from jax.experimental.pallas import tpu as pltpu
from jax.sharding import PartitionSpec as P

GROUP = 16
MODES = 16
SUB = 128
LANES = 128
BLK = 256
MESH = pl.DeviceIdType.MESH
F32 = jnp.float32
BF16 = jnp.bfloat16


def dot(a, b):
    return jnp.dot(a, b, preferred_element_type=F32)


def split(a):
    high = a.astype(BF16)
    return high, (a - high.astype(F32)).astype(BF16)


def kernel(
    lines,
    q_hbm,
    k_hbm,
    v_hbm,
    w_hbm,
    rates_ref,
    residues_ref,
    skip_ref,
    o_hbm,
    qb,
    kb,
    vb,
    ub,
    wb,
    ob,
    mixed,
    local,
    d_tab,
    a_hi,
    a_lo,
    h_pad,
    toep,
    sums,
    rate3,
    s_send,
    s_recv,
    l_send,
    l_recv,
    x_send,
    x_recv,
    far_s,
    far_r,
    near_s,
    near_r,
    lsem,
    osem,
    s_ss,
    s_rs,
    l_ss,
    l_rs,
    x_ss,
    x_rs,
    far_ss,
    far_rs,
    near_ss,
    near_rs,
):
    rows, chans = ub.shape
    subs = rows // SUB
    groups = chans // GROUP
    blocks = chans // BLK
    half = chans // 2
    per_line = s_send.shape[0]
    own = s_send.shape[1]

    ctx, tp = lax.axis_index("ctx"), lax.axis_index("tp")
    mx, mj = lax.div(ctx, per_line), lax.rem(ctx, per_line)
    right, left = lax.rem(tp + 1, 4), lax.rem(tp + 3, 4)
    sides = ((ctx, right), (ctx, left))

    def peer_j(k):
        return lax.rem(mj + k, per_line)

    def peer_x(k):
        return lax.rem(mx + k, lines)

    barrier = pltpu.get_barrier_semaphore()
    for k in range(1, per_line):
        pl.semaphore_signal(
            barrier, inc=1, device_id=(mx * per_line + peer_j(k), tp), device_id_type=MESH
        )
    for k in range(1, lines):
        pl.semaphore_signal(
            barrier, inc=1, device_id=(peer_x(k) * per_line + mj, tp), device_id_type=MESH
        )
    for side in sides:
        pl.semaphore_signal(barrier, inc=1, device_id=side, device_id_type=MESH)

    loads = [
        pltpu.make_async_copy(k_hbm, kb, lsem.at[0]),
        pltpu.make_async_copy(v_hbm, vb, lsem.at[1]),
        pltpu.make_async_copy(q_hbm, qb, lsem.at[2]),
    ]
    w_loads = {}
    for r in (2, 1, 3, 0):
        start = pl.multiple_of(lax.rem(tp + r, 4) * chans, chans)
        w_loads[r] = pltpu.make_async_copy(
            w_hbm.at[:, pl.ds(start, chans)], wb.at[r], lsem.at[3 + r]
        )
    for load in loads:
        load.start()
    for load in w_loads.values():
        load.start()

    rates, residues = rates_ref[...].T, residues_ref[...].T
    pick = lax.broadcasted_iota(jnp.int32, (chans, MODES), 1) == (
        lax.broadcasted_iota(jnp.int32, (chans, MODES), 0) & (MODES - 1)
    )

    def column(a):
        spread = jnp.broadcast_to(a[:, None, :], (groups, MODES, MODES)).reshape(chans, MODES)
        return jnp.sum(jnp.where(pick, spread, 0.0), axis=1, keepdims=True)

    rate_col, residue_col = column(rates), column(residues)
    lag = lax.broadcasted_iota(jnp.int32, (chans, SUB), 1).astype(F32)
    decay_in = jnp.exp(-rate_col * (SUB - 1.0 - lag))
    high, low = split(decay_in)
    d_tab[:, :SUB] = high
    d_tab[:, SUB:] = low
    spread = (
        lax.shift_right_logical(lax.broadcasted_iota(jnp.int32, (groups, chans), 1), 4)
        == lax.broadcasted_iota(jnp.int32, (groups, chans), 0)
    ).astype(F32)
    rate_row = jnp.dot(
        rates_ref[...], spread, precision=lax.Precision.HIGHEST, preferred_element_type=F32
    )
    for k in range(chans // LANES):
        rate3[:, k, :] = rate_row[:, k * LANES : (k + 1) * LANES]
    same_group = lax.shift_right_logical(
        lax.broadcasted_iota(jnp.int32, (BLK, BLK), 0), 4
    ) == lax.shift_right_logical(lax.broadcasted_iota(jnp.int32, (BLK, BLK), 1), 4)
    diag = same_group.astype(F32)

    loads[0].wait()
    loads[1].wait()
    for j in range(subs):
        at = pl.ds(j * SUB, SUB)
        for b in range(blocks):
            cols = pl.ds(b * BLK, BLK)
            u = (kb[at, cols].astype(F32) * vb[at, cols].astype(F32)).astype(BF16)
            ub[at, cols] = u
            full = dot(d_tab[cols, :], jnp.concatenate([u, u], axis=0))
            sums[j, :, cols] = jnp.sum((full * diag).reshape(BLK // MODES, MODES, BLK), axis=0)
    step_decay = jnp.exp(-rate_row * SUB)
    state = jnp.zeros_like(rate_row)
    for j in range(subs):
        following = step_decay * state + sums[j]
        sums[j] = state
        state = following
    for k in range(chans // LANES):
        piece = state[:, k * LANES : (k + 1) * LANES]
        s_send[:, :, k, :] = piece.reshape(per_line, own, LANES)

    pl.semaphore_wait(barrier, per_line - 1 + lines - 1 + 2)

    def s_copy(k):
        to = peer_j(k)
        return pltpu.make_async_remote_copy(
            src_ref=s_send.at[to],
            dst_ref=s_recv.at[mj],
            send_sem=s_ss.at[k],
            recv_sem=s_rs.at[k],
            device_id=(mx * per_line + to, tp),
            device_id_type=MESH,
        )

    def l_copy(k):
        return pltpu.make_async_remote_copy(
            src_ref=l_send,
            dst_ref=l_recv.at[mx],
            send_sem=l_ss.at[k],
            recv_sem=l_rs.at[k],
            device_id=(peer_x(k) * per_line + mj, tp),
            device_id_type=MESH,
        )

    def x_copy(k):
        to = peer_j(k)
        return pltpu.make_async_remote_copy(
            src_ref=x_send.at[to],
            dst_ref=x_recv.at[mj],
            send_sem=x_ss.at[k],
            recv_sem=x_rs.at[k],
            device_id=(mx * per_line + to, tp),
            device_id_type=MESH,
        )

    for k in range(1, per_line):
        s_copy(k).start()
    s_recv[mj] = s_send[mj]

    taps = jnp.sum((decay_in * residue_col).reshape(groups, MODES, SUB), axis=1)
    h_pad[:, :SUB] = taps
    h_pad[:, SUB:] = jnp.zeros_like(taps)

    def build(n, carry):
        for side in range(2):
            row = jnp.broadcast_to(h_pad[pl.ds(2 * n + side, 1), :], (SUB, 2 * SUB))
            turned = pltpu.roll(row, SUB + 1, 1, stride=1, stride_axis=0)
            toep[n, :, side * SUB : (side + 1) * SUB] = turned[:, :SUB].astype(BF16)
        return carry

    lax.fori_loop(0, groups // 2, build, 0)

    for k in range(1, per_line):
        s_copy(k).wait_recv()
    my_rate = rate3[pl.ds(mj * own, own)]
    block_decay = jnp.exp(-my_rate * rows)
    total = jnp.zeros_like(my_rate)
    for j in range(per_line):
        x_send[j] = total
        total = block_decay * total + s_recv[j]
    l_send[...] = total
    for k in range(1, lines):
        l_copy(k).start()

    def inside(n, carry):
        j, b = lax.div(n, blocks), lax.rem(n, blocks)
        at = pl.ds(pl.multiple_of(j * SUB, SUB), SUB)
        cols = pl.ds(pl.multiple_of(b * BLK, BLK), BLK)
        u = ub[at, cols]
        acc = skip_ref[:, cols] * u.astype(F32)
        lane_group = lax.shift_right_logical(lax.broadcasted_iota(jnp.int32, (1, BLK), 1), 4)
        for pair in range(BLK // GROUP // 2):
            masked = [
                u * (lane_group == 2 * pair + side).astype(F32).astype(BF16) for side in range(2)
            ]
            acc += dot(toep[b * (BLK // GROUP // 2) + pair], jnp.concatenate(masked, axis=0))
        local[at, cols] = acc
        return carry

    first_part = subs * blocks // 2
    lax.fori_loop(0, first_part, inside, 0)

    for k in range(1, lines):
        l_copy(k).wait_recv()
    entering = jnp.zeros_like(total)
    for other in range(lines):
        distance = mx - 1 - other
        weight = jnp.exp(-my_rate * (jnp.maximum(distance, 0) * (per_line * rows)).astype(F32))
        entering += jnp.where(distance >= 0, weight * l_recv[other], 0.0)
    for j in range(per_line):
        x_send[j] = x_send[j] + entering
        entering = entering * block_decay
    for k in range(1, per_line):
        x_copy(k).start()
    x_recv[mj] = x_send[mj]

    high, low = split((residue_col * jnp.exp(-rate_col * (lag + 1.0))).T)
    a_hi[...] = high
    a_lo[...] = low
    lax.fori_loop(first_part, subs * blocks, inside, 0)
    loads[2].wait()
    for k in range(1, per_line):
        x_copy(k).wait_recv()

    def far_copy(way, j):
        return pltpu.make_async_remote_copy(
            src_ref=far_s.at[way, j],
            dst_ref=far_r.at[way, j],
            send_sem=far_ss.at[way, j],
            recv_sem=far_rs.at[way, j],
            device_id=sides[way],
            device_id_type=MESH,
        )

    def near_copy(way, part, j):
        return pltpu.make_async_remote_copy(
            src_ref=near_s.at[way, part, j],
            dst_ref=near_r.at[way, part, j],
            send_sem=near_ss.at[way, part, j],
            recv_sem=near_rs.at[way, part, j],
            device_id=sides[way],
            device_id_type=MESH,
        )

    def project(j, r, part):
        at = pl.ds(pl.multiple_of(j * SUB, SUB), SUB)
        return dot(mixed[at, :], wb[r, :, part * half : (part + 1) * half])

    w_loads[2].wait()
    entry = jnp.concatenate(
        [x_recv[:, :, k, :].reshape(MODES, LANES) for k in range(chans // LANES)], axis=1
    )
    diag_bf = diag.astype(BF16)

    def far_step(j, carry):
        at = pl.ds(pl.multiple_of(j * SUB, SUB), SUB)
        start = jnp.exp(-rate_row * (j * SUB).astype(F32)) * entry + sums[j]
        x_hi, x_lo = split(start)
        for b in range(blocks):
            cols = slice(b * BLK, (b + 1) * BLK)
            wide_hi = jnp.concatenate([x_hi[:, cols]] * (BLK // MODES), axis=0) * diag_bf
            wide_lo = jnp.concatenate([x_lo[:, cols]] * (BLK // MODES), axis=0) * diag_bf
            past = dot(a_hi[:, cols], wide_hi) + dot(a_lo[:, cols], wide_hi)
            past += dot(a_hi[:, cols], wide_lo)
            mixed[at, cols] = (qb[at, cols].astype(F32) * (local[at, cols] + past)).astype(BF16)
        for way in range(2):
            far_s[way, j] = project(j, 2, way).astype(BF16)
            far_copy(way, j).start()
        return carry

    lax.fori_loop(0, subs, far_step, 0)
    w_loads[1].wait()
    w_loads[3].wait()

    def direct_step(j, carry):
        for way in range(2):
            near_s[way, 1 - way, j] = project(j, 1 + 2 * way, 1 - way).astype(BF16)
            near_copy(way, 1 - way, j).start()
        return carry

    lax.fori_loop(0, subs, direct_step, 0)

    def joint_step(j, carry):
        for way in range(2):
            part = project(j, 1 + 2 * way, way)
            far_copy(way, j).wait_recv()
            near_s[way, way, j] = (part + far_r[way, j].astype(F32)).astype(BF16)
            near_copy(way, way, j).start()
        return carry

    lax.fori_loop(0, subs, joint_step, 0)
    w_loads[0].wait()

    def out_copy(j):
        at = pl.ds(pl.multiple_of(j * SUB, SUB), SUB)
        return pltpu.make_async_copy(ob.at[at], o_hbm.at[at], osem.at[j])

    def last_step(j, carry):
        at = pl.ds(pl.multiple_of(j * SUB, SUB), SUB)
        for part in range(2):
            mine = project(j, 0, part)
            near_copy(0, part, j).wait_recv()
            near_copy(1, part, j).wait_recv()
            mine += near_r[0, part, j].astype(F32) + near_r[1, part, j].astype(F32)
            ob[at, part * half : (part + 1) * half] = mine.astype(BF16)
        out_copy(j).start()
        return carry

    lax.fori_loop(0, subs, last_step, 0)

    def drain(j, carry):
        for way in range(2):
            far_copy(way, j).wait_send()
            for part in range(2):
                near_copy(way, part, j).wait_send()
        out_copy(j).wait()
        return carry

    lax.fori_loop(0, subs, drain, 0)
    for k in range(1, per_line):
        s_copy(k).wait_send()
        x_copy(k).wait_send()
    for k in range(1, lines):
        l_copy(k).wait_send()


def shards(lines, query, key_in, value, rates, residues, skip_gain, out_weight):
    rows, chans = query.shape
    groups = chans // GROUP
    subs = rows // SUB
    half = chans // 2
    per_line = lax.axis_size("ctx") // lines
    own = MODES // per_line
    tile = chans // LANES
    hbm = pl.BlockSpec(memory_space=pl.ANY)
    vmem = pl.BlockSpec(memory_space=pltpu.VMEM)
    dma = pltpu.SemaphoreType.DMA
    return pl.pallas_call(
        functools.partial(kernel, lines),
        name="hyena",
        out_shape=jax.ShapeDtypeStruct((rows, chans), BF16),
        in_specs=[hbm, hbm, hbm, hbm, vmem, vmem, vmem],
        out_specs=hbm,
        scratch_shapes=[
            pltpu.VMEM((rows, chans), BF16),
            pltpu.VMEM((rows, chans), BF16),
            pltpu.VMEM((rows, chans), BF16),
            pltpu.VMEM((rows, chans), BF16),
            pltpu.VMEM((4, chans, chans), BF16),
            pltpu.VMEM((rows, chans), BF16),
            pltpu.VMEM((rows, chans), BF16),
            pltpu.VMEM((rows, chans), F32),
            pltpu.VMEM((chans, 2 * SUB), BF16),
            pltpu.VMEM((SUB, chans), BF16),
            pltpu.VMEM((SUB, chans), BF16),
            pltpu.VMEM((groups, 2 * SUB), F32),
            pltpu.VMEM((groups // 2, SUB, 2 * SUB), BF16),
            pltpu.VMEM((subs, MODES, chans), F32),
            pltpu.VMEM((MODES, tile, LANES), F32),
            pltpu.VMEM((per_line, own, tile, LANES), F32),
            pltpu.VMEM((per_line, own, tile, LANES), F32),
            pltpu.VMEM((own, tile, LANES), F32),
            pltpu.VMEM((lines, own, tile, LANES), F32),
            pltpu.VMEM((per_line, own, tile, LANES), F32),
            pltpu.VMEM((per_line, own, tile, LANES), F32),
            pltpu.VMEM((2, subs, SUB, half), BF16),
            pltpu.VMEM((2, subs, SUB, half), BF16),
            pltpu.VMEM((2, 2, subs, SUB, half), BF16),
            pltpu.VMEM((2, 2, subs, SUB, half), BF16),
            dma((7,)),
            dma((subs,)),
            dma((per_line,)),
            dma((per_line,)),
            dma((lines,)),
            dma((lines,)),
            dma((per_line,)),
            dma((per_line,)),
            dma((2, subs)),
            dma((2, subs)),
            dma((2, 2, subs)),
            dma((2, 2, subs)),
        ],
        compiler_params=pltpu.CompilerParams(
            collective_id=0, has_side_effects=True, vmem_limit_bytes=56 * 1024 * 1024
        ),
    )(query, key_in, value, out_weight, rates.T, residues.T, skip_gain[None, :])


def solution(mesh):
    in_specs = (
        P("ctx", "tp"),
        P("ctx", "tp"),
        P("ctx", "tp"),
        P("tp", None),
        P("tp", None),
        P("tp"),
        P("tp", None),
    )
    lines = max(1, mesh.shape["ctx"] // MODES)
    return jax.shard_map(
        functools.partial(shards, lines),
        mesh=mesh,
        in_specs=in_specs,
        out_specs=P("ctx", "tp"),
        check_vma=False,
    )
```

```python
import functools

import jax
import jax.numpy as jnp
from jax import lax
from jax.experimental import pallas as pl
from jax.experimental.pallas import tpu as pltpu
from jax.sharding import PartitionSpec as P

GROUP = 16
MODES = 16
SUB = 128
LANES = 128
BLK = 256
MESH = pl.DeviceIdType.MESH
F32 = jnp.float32
BF16 = jnp.bfloat16


def dot(a, b):
    return jnp.dot(a, b, preferred_element_type=F32)


def split(a):
    high = a.astype(BF16)
    return high, (a - high.astype(F32)).astype(BF16)


def kernel(
    lines,
    q_hbm,
    k_hbm,
    v_hbm,
    w_hbm,
    rates_ref,
    residues_ref,
    skip_ref,
    ob,
    qb,
    kb,
    vb,
    ub,
    wb,
    mixed,
    local,
    d_tab,
    a_hi,
    a_lo,
    h_pad,
    toep,
    sums,
    rate3,
    s_send,
    s_recv,
    l_send,
    l_recv,
    x_send,
    x_recv,
    far_s,
    far_r,
    near_s,
    near_r,
    lsem,
    s_ss,
    s_rs,
    l_ss,
    l_rs,
    x_ss,
    x_rs,
    far_ss,
    far_rs,
    near_ss,
    near_rs,
):
    rows, chans = ub.shape
    subs = rows // SUB
    groups = chans // GROUP
    blocks = chans // BLK
    half = chans // 2
    per_line = s_send.shape[0]
    own = s_send.shape[1]

    ctx, tp = lax.axis_index("ctx"), lax.axis_index("tp")
    mx, mj = lax.div(ctx, per_line), lax.rem(ctx, per_line)
    right, left = lax.rem(tp + 1, 4), lax.rem(tp + 3, 4)
    sides = ((ctx, right), (ctx, left))

    order = sorted(range(1, per_line), key=lambda k: abs(2 * k - per_line))

    def peer_j(k):
        return lax.rem(mj + k, per_line)

    def peer_x(k):
        return lax.rem(mx + k, lines)

    barrier = pltpu.get_barrier_semaphore()
    for k in range(1, per_line):
        pl.semaphore_signal(
            barrier, inc=1, device_id=(mx * per_line + peer_j(k), tp), device_id_type=MESH
        )
    for k in range(1, lines):
        pl.semaphore_signal(
            barrier, inc=1, device_id=(peer_x(k) * per_line + mj, tp), device_id_type=MESH
        )
    for side in sides:
        pl.semaphore_signal(barrier, inc=1, device_id=side, device_id_type=MESH)

    loads = [
        pltpu.make_async_copy(k_hbm, kb, lsem.at[0]),
        pltpu.make_async_copy(v_hbm, vb, lsem.at[1]),
        pltpu.make_async_copy(q_hbm, qb, lsem.at[2]),
    ]
    w_loads = {}
    for r in (2, 1, 3, 0):
        start = pl.multiple_of(lax.rem(tp + r, 4) * chans, chans)
        w_loads[r] = pltpu.make_async_copy(
            w_hbm.at[:, pl.ds(start, chans)], wb.at[r], lsem.at[3 + r]
        )
    loads[0].start()
    loads[1].start()

    rates, residues = rates_ref[...].T, residues_ref[...].T
    pick = lax.broadcasted_iota(jnp.int32, (chans, MODES), 1) == (
        lax.broadcasted_iota(jnp.int32, (chans, MODES), 0) & (MODES - 1)
    )

    def column(a):
        spread = jnp.broadcast_to(a[:, None, :], (groups, MODES, MODES)).reshape(chans, MODES)
        return jnp.sum(jnp.where(pick, spread, 0.0), axis=1, keepdims=True)

    rate_col, residue_col = column(rates), column(residues)
    lag = lax.broadcasted_iota(jnp.int32, (chans, SUB), 1).astype(F32)
    decay_in = jnp.exp(-rate_col * (SUB - 1.0 - lag))
    high, low = split(decay_in)
    d_tab[:, :SUB] = high
    d_tab[:, SUB:] = low
    spread = (
        lax.shift_right_logical(lax.broadcasted_iota(jnp.int32, (groups, chans), 1), 4)
        == lax.broadcasted_iota(jnp.int32, (groups, chans), 0)
    ).astype(F32)
    rate_row = jnp.dot(
        rates_ref[...], spread, precision=lax.Precision.HIGHEST, preferred_element_type=F32
    )
    for k in range(chans // LANES):
        rate3[:, k, :] = rate_row[:, k * LANES : (k + 1) * LANES]
    same_group = lax.shift_right_logical(
        lax.broadcasted_iota(jnp.int32, (BLK, BLK), 0), 4
    ) == lax.shift_right_logical(lax.broadcasted_iota(jnp.int32, (BLK, BLK), 1), 4)
    diag = same_group.astype(F32)

    loads[0].wait()
    loads[1].wait()
    loads[2].start()
    for load in w_loads.values():
        load.start()
    for j in range(subs):
        at = pl.ds(j * SUB, SUB)
        for b in range(blocks):
            cols = pl.ds(b * BLK, BLK)
            u = (kb[at, cols].astype(F32) * vb[at, cols].astype(F32)).astype(BF16)
            ub[at, cols] = u
            full = dot(d_tab[cols, :], jnp.concatenate([u, u], axis=0))
            sums[j, :, cols] = jnp.sum((full * diag).reshape(BLK // MODES, MODES, BLK), axis=0)
    step_decay = jnp.exp(-rate_row * SUB)
    state = jnp.zeros_like(rate_row)
    for j in range(subs):
        following = step_decay * state + sums[j]
        sums[j] = state
        state = following
    for k in range(chans // LANES):
        piece = state[:, k * LANES : (k + 1) * LANES]
        s_send[:, :, k, :] = piece.reshape(per_line, own, LANES)

    pl.semaphore_wait(barrier, per_line - 1 + lines - 1 + 2)

    def s_copy(k):
        to = peer_j(k)
        return pltpu.make_async_remote_copy(
            src_ref=s_send.at[to],
            dst_ref=s_recv.at[mj],
            send_sem=s_ss.at[k],
            recv_sem=s_rs.at[k],
            device_id=(mx * per_line + to, tp),
            device_id_type=MESH,
        )

    def l_copy(k):
        return pltpu.make_async_remote_copy(
            src_ref=l_send,
            dst_ref=l_recv.at[mx],
            send_sem=l_ss.at[k],
            recv_sem=l_rs.at[k],
            device_id=(peer_x(k) * per_line + mj, tp),
            device_id_type=MESH,
        )

    def x_copy(k):
        to = peer_j(k)
        return pltpu.make_async_remote_copy(
            src_ref=x_send.at[to],
            dst_ref=x_recv.at[mj],
            send_sem=x_ss.at[k],
            recv_sem=x_rs.at[k],
            device_id=(mx * per_line + to, tp),
            device_id_type=MESH,
        )

    for k in order:
        s_copy(k).start()
    s_recv[mj] = s_send[mj]

    taps = jnp.sum((decay_in * residue_col).reshape(groups, MODES, SUB), axis=1)
    h_pad[:, :SUB] = taps
    h_pad[:, SUB:] = jnp.zeros_like(taps)

    def build(n, carry):
        for side in range(2):
            row = jnp.broadcast_to(h_pad[pl.ds(2 * n + side, 1), :], (SUB, 2 * SUB))
            turned = pltpu.roll(row, SUB + 1, 1, stride=1, stride_axis=0)
            toep[n, :, side * SUB : (side + 1) * SUB] = turned[:, :SUB].astype(BF16)
        return carry

    lax.fori_loop(0, groups // 2, build, 0)

    my_rate = rate3[pl.ds(mj * own, own)]
    block_decay = jnp.exp(-my_rate * rows)
    weights = []
    for other in range(lines):
        distance = mx - 1 - other
        span = jnp.maximum(distance, 0) * (per_line * rows)
        weights.append(jnp.where(distance >= 0, jnp.exp(-my_rate * span.astype(F32)), 0.0))
    for k in range(1, per_line):
        s_copy(k).wait_recv()
    total = jnp.zeros_like(my_rate)
    for j in range(per_line):
        x_send[j] = total
        total = block_decay * total + s_recv[j]
    l_send[...] = total
    l_recv[mx] = total
    for k in range(1, lines):
        l_copy(k).start()

    def inside(n, carry):
        j, b = lax.div(n, blocks), lax.rem(n, blocks)
        at = pl.ds(pl.multiple_of(j * SUB, SUB), SUB)
        cols = pl.ds(pl.multiple_of(b * BLK, BLK), BLK)
        u = ub[at, cols]
        acc = skip_ref[:, cols] * u.astype(F32)
        lane_group = lax.shift_right_logical(lax.broadcasted_iota(jnp.int32, (1, BLK), 1), 4)
        for pair in range(BLK // GROUP // 2):
            masked = [
                u * (lane_group == 2 * pair + side).astype(F32).astype(BF16) for side in range(2)
            ]
            acc += dot(toep[b * (BLK // GROUP // 2) + pair], jnp.concatenate(masked, axis=0))
        local[at, cols] = acc
        return carry

    first_part = subs * blocks // 2
    lax.fori_loop(0, first_part, inside, 0)

    for k in range(1, lines):
        l_copy(k).wait_recv()
    entering = jnp.zeros_like(total)
    for other in range(lines):
        entering += weights[other] * l_recv[other]
    for j in range(per_line):
        x_send[j] = x_send[j] + entering
        entering = entering * block_decay
    for k in order:
        x_copy(k).start()
    x_recv[mj] = x_send[mj]

    high, low = split((residue_col * jnp.exp(-rate_col * (lag + 1.0))).T)
    a_hi[...] = high
    a_lo[...] = low
    lax.fori_loop(first_part, subs * blocks, inside, 0)
    loads[2].wait()
    for k in range(1, per_line):
        x_copy(k).wait_recv()

    def far_copy(way, j):
        return pltpu.make_async_remote_copy(
            src_ref=far_s.at[way, j],
            dst_ref=far_r.at[way, j],
            send_sem=far_ss.at[way, j],
            recv_sem=far_rs.at[way, j],
            device_id=sides[way],
            device_id_type=MESH,
        )

    def near_copy(way, part, j):
        return pltpu.make_async_remote_copy(
            src_ref=near_s.at[way, part, j],
            dst_ref=near_r.at[way, part, j],
            send_sem=near_ss.at[way, part, j],
            recv_sem=near_rs.at[way, part, j],
            device_id=sides[way],
            device_id_type=MESH,
        )

    def project(j, r, part):
        at = pl.ds(pl.multiple_of(j * SUB, SUB), SUB)
        return dot(mixed[at, :], wb[r, :, part * half : (part + 1) * half])

    w_loads[2].wait()
    entry = jnp.concatenate(
        [x_recv[:, :, k, :].reshape(MODES, LANES) for k in range(chans // LANES)], axis=1
    )
    diag_bf = diag.astype(BF16)

    def far_step(j, carry):
        at = pl.ds(pl.multiple_of(j * SUB, SUB), SUB)
        start = jnp.exp(-rate_row * (j * SUB).astype(F32)) * entry + sums[j]
        x_hi, x_lo = split(start)
        for b in range(blocks):
            cols = slice(b * BLK, (b + 1) * BLK)
            wide_hi = jnp.concatenate([x_hi[:, cols]] * (BLK // MODES), axis=0) * diag_bf
            wide_lo = jnp.concatenate([x_lo[:, cols]] * (BLK // MODES), axis=0) * diag_bf
            past = dot(a_hi[:, cols], wide_hi) + dot(a_lo[:, cols], wide_hi)
            past += dot(a_hi[:, cols], wide_lo)
            mixed[at, cols] = (qb[at, cols].astype(F32) * (local[at, cols] + past)).astype(BF16)
        for way in range(2):
            far_s[way, j] = project(j, 2, way).astype(BF16)
            far_copy(way, j).start()
        return carry

    lax.fori_loop(0, subs, far_step, 0)
    w_loads[1].wait()
    w_loads[3].wait()

    def direct_step(j, carry):
        for way in range(2):
            near_s[way, 1 - way, j] = project(j, 1 + 2 * way, 1 - way).astype(BF16)
            near_copy(way, 1 - way, j).start()
        return carry

    lax.fori_loop(0, subs, direct_step, 0)

    def joint_step(j, carry):
        for way in range(2):
            part = project(j, 1 + 2 * way, way)
            far_copy(way, j).wait_recv()
            near_s[way, way, j] = (part + far_r[way, j].astype(F32)).astype(BF16)
            near_copy(way, way, j).start()
        return carry

    lax.fori_loop(0, subs, joint_step, 0)
    w_loads[0].wait()

    def last_step(j, carry):
        at = pl.ds(pl.multiple_of(j * SUB, SUB), SUB)
        for part in range(2):
            mine = project(j, 0, part)
            near_copy(0, part, j).wait_recv()
            near_copy(1, part, j).wait_recv()
            mine += near_r[0, part, j].astype(F32) + near_r[1, part, j].astype(F32)
            ob[at, part * half : (part + 1) * half] = mine.astype(BF16)
        return carry

    lax.fori_loop(0, subs, last_step, 0)

    def drain(j, carry):
        for way in range(2):
            far_copy(way, j).wait_send()
            for part in range(2):
                near_copy(way, part, j).wait_send()
        return carry

    lax.fori_loop(0, subs, drain, 0)
    for k in range(1, per_line):
        s_copy(k).wait_send()
        x_copy(k).wait_send()
    for k in range(1, lines):
        l_copy(k).wait_send()


def shards(lines, query, key_in, value, rates, residues, skip_gain, out_weight):
    rows, chans = query.shape
    groups = chans // GROUP
    subs = rows // SUB
    half = chans // 2
    per_line = lax.axis_size("ctx") // lines
    own = MODES // per_line
    tile = chans // LANES
    hbm = pl.BlockSpec(memory_space=pl.ANY)
    vmem = pl.BlockSpec(memory_space=pltpu.VMEM)
    dma = pltpu.SemaphoreType.DMA
    return pl.pallas_call(
        functools.partial(kernel, lines),
        name="hyena",
        out_shape=pltpu.VMEM((rows, chans), BF16),
        in_specs=[hbm, hbm, hbm, hbm, vmem, vmem, vmem],
        out_specs=vmem,
        scratch_shapes=[
            pltpu.VMEM((rows, chans), BF16),
            pltpu.VMEM((rows, chans), BF16),
            pltpu.VMEM((rows, chans), BF16),
            pltpu.VMEM((rows, chans), BF16),
            pltpu.VMEM((4, chans, chans), BF16),
            pltpu.VMEM((rows, chans), BF16),
            pltpu.VMEM((rows, chans), F32),
            pltpu.VMEM((chans, 2 * SUB), BF16),
            pltpu.VMEM((SUB, chans), BF16),
            pltpu.VMEM((SUB, chans), BF16),
            pltpu.VMEM((groups, 2 * SUB), F32),
            pltpu.VMEM((groups // 2, SUB, 2 * SUB), BF16),
            pltpu.VMEM((subs, MODES, chans), F32),
            pltpu.VMEM((MODES, tile, LANES), F32),
            pltpu.VMEM((per_line, own, tile, LANES), F32),
            pltpu.VMEM((per_line, own, tile, LANES), F32),
            pltpu.VMEM((own, tile, LANES), F32),
            pltpu.VMEM((lines, own, tile, LANES), F32),
            pltpu.VMEM((per_line, own, tile, LANES), F32),
            pltpu.VMEM((per_line, own, tile, LANES), F32),
            pltpu.VMEM((2, subs, SUB, half), BF16),
            pltpu.VMEM((2, subs, SUB, half), BF16),
            pltpu.VMEM((2, 2, subs, SUB, half), BF16),
            pltpu.VMEM((2, 2, subs, SUB, half), BF16),
            dma((7,)),
            dma((per_line,)),
            dma((per_line,)),
            dma((lines,)),
            dma((lines,)),
            dma((per_line,)),
            dma((per_line,)),
            dma((2, subs)),
            dma((2, subs)),
            dma((2, 2, subs)),
            dma((2, 2, subs)),
        ],
        compiler_params=pltpu.CompilerParams(
            collective_id=0, has_side_effects=True, vmem_limit_bytes=56 * 1024 * 1024
        ),
    )(query, key_in, value, out_weight, rates.T, residues.T, skip_gain[None, :])


def solution(mesh):
    in_specs = (
        P("ctx", "tp"),
        P("ctx", "tp"),
        P("ctx", "tp"),
        P("tp", None),
        P("tp", None),
        P("tp"),
        P("tp", None),
    )
    lines = max(1, mesh.shape["ctx"] // MODES)
    return jax.shard_map(
        functools.partial(shards, lines),
        mesh=mesh,
        in_specs=in_specs,
        out_specs=P("ctx", "tp"),
        check_vma=False,
    )
```

```python
import functools

import jax
import jax.numpy as jnp
from jax import lax
from jax.experimental import pallas as pl
from jax.experimental.pallas import tpu as pltpu
from jax.sharding import PartitionSpec as P

GROUP = 16
MODES = 16
SUB = 128
LANES = 128
BLK = 256
STEP = 64
MESH = pl.DeviceIdType.MESH
F32 = jnp.float32
BF16 = jnp.bfloat16


def dot(a, b):
    return jnp.dot(a, b, preferred_element_type=F32)


def split(a):
    high = a.astype(BF16)
    return high, (a - high.astype(F32)).astype(BF16)


def kernel(
    lines,
    q_hbm,
    k_hbm,
    v_hbm,
    w_hbm,
    rates_ref,
    residues_ref,
    skip_ref,
    ob,
    qb,
    kb,
    vb,
    ub,
    wb,
    mixed,
    local,
    d_tab,
    a_hi,
    a_lo,
    h_pad,
    toep,
    sums,
    rate3,
    s_send,
    s_recv,
    l_send,
    l_recv,
    x_send,
    x_recv,
    far_s,
    far_r,
    near_s,
    near_r,
    wp,
    pair_r,
    sum_s,
    sum_r,
    lsem,
    s_ss,
    s_rs,
    l_ss,
    l_rs,
    x_ss,
    x_rs,
    far_ss,
    far_rs,
    near_ss,
    near_rs,
    wy_ss,
    wy_rs,
    wx_ss,
    wx_rs,
    wf_ss,
    wf_rs,
    sib_ss,
    sib_rs,
    pair_ss,
    pair_rs,
    sum_ss,
    sum_rs,
):
    rows, chans = ub.shape
    subs = rows // SUB
    groups = chans // GROUP
    blocks = chans // BLK
    half = chans // 2
    per_line = s_send.shape[0]
    own = s_send.shape[1]

    ctx, tp = lax.axis_index("ctx"), lax.axis_index("tp")
    mx, mj = lax.div(ctx, per_line), lax.rem(ctx, per_line)
    right, left = lax.rem(tp + 1, 4), lax.rem(tp + 3, 4)
    sides = ((ctx, right), (ctx, left))
    odd = lax.rem(tp, 2)
    pair, opp = tp + 1 - 2 * odd, 3 - tp
    way_pair, way_opp = odd, 1 - odd
    core = lax.rem(ctx, 2)
    sibling = ctx + 1 - 2 * core
    slice_rows, piece_rows = chans // 8, chans // 16
    pieces = 4
    steps = pair_r.shape[0]
    step_rows = pair_r.shape[1]

    order = sorted(range(1, per_line), key=lambda k: abs(2 * k - per_line))

    def peer_j(k):
        return lax.rem(mj + k, per_line)

    def peer_x(k):
        return lax.rem(mx + k, lines)

    barrier = pltpu.get_barrier_semaphore()
    for k in range(1, per_line):
        pl.semaphore_signal(
            barrier, inc=1, device_id=(mx * per_line + peer_j(k), tp), device_id_type=MESH
        )
    for k in range(1, lines):
        pl.semaphore_signal(
            barrier, inc=1, device_id=(peer_x(k) * per_line + mj, tp), device_id_type=MESH
        )
    for side in sides:
        pl.semaphore_signal(barrier, inc=1, device_id=side, device_id_type=MESH)

    loads = [
        pltpu.make_async_copy(k_hbm, kb, lsem.at[0]),
        pltpu.make_async_copy(v_hbm, vb, lsem.at[1]),
        pltpu.make_async_copy(q_hbm, qb, lsem.at[2]),
    ]
    w_loads = {}
    for r in (2, 1, 3, 0):
        start = pl.multiple_of(lax.rem(tp + r, 4) * chans, chans)
        w_loads[r] = pltpu.make_async_copy(
            w_hbm.at[:, pl.ds(start, chans)], wb.at[r], lsem.at[3 + r]
        )
    loads[0].start()
    loads[1].start()

    rates, residues = rates_ref[...].T, residues_ref[...].T
    pick = lax.broadcasted_iota(jnp.int32, (chans, MODES), 1) == (
        lax.broadcasted_iota(jnp.int32, (chans, MODES), 0) & (MODES - 1)
    )

    def column(a):
        spread = jnp.broadcast_to(a[:, None, :], (groups, MODES, MODES)).reshape(chans, MODES)
        return jnp.sum(jnp.where(pick, spread, 0.0), axis=1, keepdims=True)

    rate_col, residue_col = column(rates), column(residues)
    lag = lax.broadcasted_iota(jnp.int32, (chans, SUB), 1).astype(F32)
    decay_in = jnp.exp(-rate_col * (SUB - 1.0 - lag))
    high, low = split(decay_in)
    d_tab[:, :SUB] = high
    d_tab[:, SUB:] = low
    spread = (
        lax.shift_right_logical(lax.broadcasted_iota(jnp.int32, (groups, chans), 1), 4)
        == lax.broadcasted_iota(jnp.int32, (groups, chans), 0)
    ).astype(F32)
    rate_row = jnp.dot(
        rates_ref[...], spread, precision=lax.Precision.HIGHEST, preferred_element_type=F32
    )
    for k in range(chans // LANES):
        rate3[:, k, :] = rate_row[:, k * LANES : (k + 1) * LANES]
    same_group = lax.shift_right_logical(
        lax.broadcasted_iota(jnp.int32, (BLK, BLK), 0), 4
    ) == lax.shift_right_logical(lax.broadcasted_iota(jnp.int32, (BLK, BLK), 1), 4)
    diag = same_group.astype(F32)

    loads[0].wait()
    loads[1].wait()
    loads[2].start()
    for load in w_loads.values():
        load.start()
    for j in range(subs):
        at = pl.ds(j * SUB, SUB)
        for b in range(blocks):
            cols = pl.ds(b * BLK, BLK)
            u = (kb[at, cols].astype(F32) * vb[at, cols].astype(F32)).astype(BF16)
            ub[at, cols] = u
            full = dot(d_tab[cols, :], jnp.concatenate([u, u], axis=0))
            sums[j, :, cols] = jnp.sum((full * diag).reshape(BLK // MODES, MODES, BLK), axis=0)
    step_decay = jnp.exp(-rate_row * SUB)
    state = jnp.zeros_like(rate_row)
    for j in range(subs):
        following = step_decay * state + sums[j]
        sums[j] = state
        state = following
    for k in range(chans // LANES):
        piece = state[:, k * LANES : (k + 1) * LANES]
        s_send[:, :, k, :] = piece.reshape(per_line, own, LANES)

    pl.semaphore_wait(barrier, per_line - 1 + lines - 1 + 2)

    def s_copy(k):
        to = peer_j(k)
        return pltpu.make_async_remote_copy(
            src_ref=s_send.at[to],
            dst_ref=s_recv.at[mj],
            send_sem=s_ss.at[k],
            recv_sem=s_rs.at[k],
            device_id=(mx * per_line + to, tp),
            device_id_type=MESH,
        )

    def l_copy(k):
        return pltpu.make_async_remote_copy(
            src_ref=l_send,
            dst_ref=l_recv.at[mx],
            send_sem=l_ss.at[k],
            recv_sem=l_rs.at[k],
            device_id=(peer_x(k) * per_line + mj, tp),
            device_id_type=MESH,
        )

    def x_copy(k):
        to = peer_j(k)
        return pltpu.make_async_remote_copy(
            src_ref=x_send.at[to],
            dst_ref=x_recv.at[mj],
            send_sem=x_ss.at[k],
            recv_sem=x_rs.at[k],
            device_id=(mx * per_line + to, tp),
            device_id_type=MESH,
        )

    def piece(k, slot, lead, size):
        start = core * (chans // 2) + slot * slice_rows + (k % 2) * piece_rows + lead
        return pl.ds(pl.multiple_of(start, piece_rows // 2), size)

    def wy_copy(k):
        block = 1 - k // 2
        column = pair if block == 0 else 3 - pair
        at = piece(k, mx, 0, piece_rows)
        return pltpu.make_async_remote_copy(
            src_ref=w_hbm.at[at, pl.ds(pl.multiple_of(column * chans, chans), chans)],
            dst_ref=wp.at[block, at],
            send_sem=wy_ss.at[k],
            recv_sem=wy_rs.at[k],
            device_id=(ctx, pair),
            device_id_type=MESH,
        )

    def x_side(way):
        return (peer_x(1 if way == 0 else lines - 1) * per_line + mj, tp)

    def wx_copy(k, way):
        ref = wp.at[1 - k // 2, piece(k, mx, 0, piece_rows)]
        return pltpu.make_async_remote_copy(
            src_ref=ref,
            dst_ref=ref,
            send_sem=wx_ss.at[k, way],
            recv_sem=wx_rs.at[k, way],
            device_id=x_side(way),
            device_id_type=MESH,
        )

    def wf_copy(k, way):
        slot = peer_x(lines - 1 if way == 0 else 1)
        ref = wp.at[1 - k // 2, piece(k, slot, way * (piece_rows // 2), piece_rows // 2)]
        return pltpu.make_async_remote_copy(
            src_ref=ref,
            dst_ref=ref,
            send_sem=wf_ss.at[k, way],
            recv_sem=wf_rs.at[k, way],
            device_id=x_side(way),
            device_id_type=MESH,
        )

    def sib_copy(block):
        ref = wp.at[block, pl.ds(pl.multiple_of(core * (chans // 2), chans // 2), chans // 2)]
        return pltpu.make_async_remote_copy(
            src_ref=ref,
            dst_ref=ref,
            send_sem=sib_ss.at[block],
            recv_sem=sib_rs.at[block],
            device_id=(sibling, tp),
            device_id_type=MESH,
        )

    def spread_piece(k):
        wy_copy(k).wait_recv()
        for way in range(2):
            wx_copy(k, way).start()

    def pass_piece(k):
        for way in range(2):
            wx_copy(k, way).wait_recv()
            wf_copy(k, way).start()

    def share_block(block):
        for k in (2 - 2 * block, 3 - 2 * block):
            for way in range(2):
                wf_copy(k, way).wait_recv()
        sib_copy(block).start()

    for k in order:
        s_copy(k).start()
    for k in range(pieces):
        wy_copy(k).start()
    s_recv[mj] = s_send[mj]

    taps = jnp.sum((decay_in * residue_col).reshape(groups, MODES, SUB), axis=1)
    h_pad[:, :SUB] = taps
    h_pad[:, SUB:] = jnp.zeros_like(taps)

    def build(n, carry):
        for side in range(2):
            row = jnp.broadcast_to(h_pad[pl.ds(2 * n + side, 1), :], (SUB, 2 * SUB))
            turned = pltpu.roll(row, SUB + 1, 1, stride=1, stride_axis=0)
            toep[n, :, side * SUB : (side + 1) * SUB] = turned[:, :SUB].astype(BF16)
        return carry

    lax.fori_loop(0, groups // 2, build, 0)

    my_rate = rate3[pl.ds(mj * own, own)]
    block_decay = jnp.exp(-my_rate * rows)
    weights = []
    for other in range(lines):
        distance = mx - 1 - other
        span = jnp.maximum(distance, 0) * (per_line * rows)
        weights.append(jnp.where(distance >= 0, jnp.exp(-my_rate * span.astype(F32)), 0.0))
    for k in range(1, per_line):
        s_copy(k).wait_recv()
    total = jnp.zeros_like(my_rate)
    for j in range(per_line):
        x_send[j] = total
        total = block_decay * total + s_recv[j]
    l_send[...] = total
    l_recv[mx] = total
    for k in range(1, lines):
        l_copy(k).start()
    spread_piece(0)

    def inside(n, carry):
        j, b = lax.div(n, blocks), lax.rem(n, blocks)
        at = pl.ds(pl.multiple_of(j * SUB, SUB), SUB)
        cols = pl.ds(pl.multiple_of(b * BLK, BLK), BLK)
        u = ub[at, cols]
        acc = skip_ref[:, cols] * u.astype(F32)
        lane_group = lax.shift_right_logical(lax.broadcasted_iota(jnp.int32, (1, BLK), 1), 4)
        for pair in range(BLK // GROUP // 2):
            masked = [
                u * (lane_group == 2 * pair + side).astype(F32).astype(BF16) for side in range(2)
            ]
            acc += dot(toep[b * (BLK // GROUP // 2) + pair], jnp.concatenate(masked, axis=0))
        local[at, cols] = acc
        return carry

    first_part = subs * blocks // 2
    lax.fori_loop(0, first_part, inside, 0)
    spread_piece(1)

    for k in range(1, lines):
        l_copy(k).wait_recv()
    entering = jnp.zeros_like(total)
    for other in range(lines):
        entering += weights[other] * l_recv[other]
    for j in range(per_line):
        x_send[j] = x_send[j] + entering
        entering = entering * block_decay
    for k in order:
        x_copy(k).start()
    x_recv[mj] = x_send[mj]

    high, low = split((residue_col * jnp.exp(-rate_col * (lag + 1.0))).T)
    a_hi[...] = high
    a_lo[...] = low
    lax.fori_loop(first_part, subs * blocks, inside, 0)
    pass_piece(0)
    pass_piece(1)
    spread_piece(2)
    loads[2].wait()
    for k in range(1, per_line):
        x_copy(k).wait_recv()

    def side_of(way):
        return (ctx, lax.rem(tp + 1 + 2 * way, 4))

    def far_copy(way):
        return pltpu.make_async_remote_copy(
            src_ref=far_s.at[way],
            dst_ref=far_r.at[way],
            send_sem=far_ss.at[way],
            recv_sem=far_rs.at[way],
            device_id=side_of(way),
            device_id_type=MESH,
        )

    def near_copy(way, part):
        return pltpu.make_async_remote_copy(
            src_ref=near_s.at[way, part],
            dst_ref=near_r.at[way, part],
            send_sem=near_ss.at[way, part],
            recv_sem=near_rs.at[way, part],
            device_id=side_of(way),
            device_id_type=MESH,
        )

    def tokens(h):
        return pl.ds(pl.multiple_of(SUB + h * step_rows, step_rows), step_rows)

    def pair_copy(h):
        return pltpu.make_async_remote_copy(
            src_ref=mixed.at[tokens(h)],
            dst_ref=pair_r.at[h],
            send_sem=pair_ss.at[h],
            recv_sem=pair_rs.at[h],
            device_id=(ctx, pair),
            device_id_type=MESH,
        )

    def sum_copy(h):
        return pltpu.make_async_remote_copy(
            src_ref=sum_s.at[h],
            dst_ref=sum_r.at[h],
            send_sem=sum_ss.at[h],
            recv_sem=sum_rs.at[h],
            device_id=(ctx, opp),
            device_id_type=MESH,
        )

    def project(r, part):
        cols = pl.ds(pl.multiple_of(part * half, half), half)
        return dot(mixed[:SUB, :], wb[r, :, cols])

    w_loads[2].wait()
    entry = jnp.concatenate(
        [x_recv[:, :, k, :].reshape(MODES, LANES) for k in range(chans // LANES)], axis=1
    )
    diag_bf = diag.astype(BF16)

    def mix(j):
        at = pl.ds(pl.multiple_of(j * SUB, SUB), SUB)
        start = jnp.exp(-rate_row * (j * SUB * 1.0)) * entry + sums[j]
        x_hi, x_lo = split(start)
        for b in range(blocks):
            cols = slice(b * BLK, (b + 1) * BLK)
            wide_hi = jnp.concatenate([x_hi[:, cols]] * (BLK // MODES), axis=0) * diag_bf
            wide_lo = jnp.concatenate([x_lo[:, cols]] * (BLK // MODES), axis=0) * diag_bf
            past = dot(a_hi[:, cols], wide_hi) + dot(a_lo[:, cols], wide_hi)
            past += dot(a_hi[:, cols], wide_lo)
            mixed[at, cols] = (qb[at, cols].astype(F32) * (local[at, cols] + past)).astype(BF16)

    per_sub = SUB // step_rows

    def mix_and_send(j):
        mix(j)
        for h in range((j - 1) * per_sub, j * per_sub):
            pair_copy(h).start()

    def direct(way):
        near_s[way, 1 - way] = project(1 + 2 * way, 1 - way).astype(BF16)
        near_copy(way, 1 - way).start()

    def joint(way):
        part = project(1 + 2 * way, way)
        far_copy(way).wait_recv()
        near_s[way, way] = (part + far_r[way].astype(F32)).astype(BF16)
        near_copy(way, way).start()

    mix(0)
    for way in range(2):
        far_s[way] = project(2, way).astype(BF16)
        far_copy(way).start()
    mix_and_send(1)
    w_loads[1].wait()
    w_loads[3].wait()
    direct(way_opp)
    for j in range(2, subs):
        mix_and_send(j)
    spread_piece(3)
    joint(way_opp)
    share_block(1)
    direct(way_pair)
    joint(way_pair)
    pass_piece(2)
    pass_piece(3)
    w_loads[0].wait()
    for part in range(2):
        cols = slice(part * half, (part + 1) * half)
        local[:SUB, cols] = project(0, part)

    opp_slot = 3 - 2 * odd
    sib_copy(1).wait_recv()

    def sum_step(h, carry):
        pair_copy(h).wait_recv()
        mine, theirs = mixed[tokens(h), :], pair_r[h]
        for part in range(2):
            cols = slice(part * half, (part + 1) * half)
            both = dot(mine, wb[opp_slot, :, cols]) + dot(theirs, wp[1, :, cols])
            sum_s[h, :, cols] = both.astype(BF16)
        sum_copy(h).start()
        return carry

    def own_step(h, carry):
        mine, theirs = mixed[tokens(h), :], pair_r[h]
        for part in range(2):
            cols = slice(part * half, (part + 1) * half)
            both = dot(mine, wb[0, :, cols]) + dot(theirs, wp[0, :, cols])
            if part == 0:
                sum_copy(h).wait_recv()
            ob[tokens(h), cols] = (both + sum_r[h, :, cols].astype(F32)).astype(BF16)
        return carry

    def both_step(h, carry):
        return own_step(h - 2, sum_step(h, carry))

    lax.fori_loop(0, 2, sum_step, 0)
    share_block(0)
    sib_copy(0).wait_recv()
    lax.fori_loop(2, steps, both_step, 0)
    lax.fori_loop(steps - 2, steps, own_step, 0)
    for part in range(2):
        cols = slice(part * half, (part + 1) * half)
        near_copy(0, part).wait_recv()
        near_copy(1, part).wait_recv()
        total = local[:SUB, cols] + near_r[0, part].astype(F32) + near_r[1, part].astype(F32)
        ob[:SUB, cols] = total.astype(BF16)

    for way in range(2):
        far_copy(way).wait_send()
        for part in range(2):
            near_copy(way, part).wait_send()
        for k in range(pieces):
            wx_copy(k, way).wait_send()
            wf_copy(k, way).wait_send()
        sib_copy(way).wait_send()
    for k in range(pieces):
        wy_copy(k).wait_send()
    for h in range(steps):
        pair_copy(h).wait_send()
        sum_copy(h).wait_send()
    for k in range(1, per_line):
        s_copy(k).wait_send()
        x_copy(k).wait_send()
    for k in range(1, lines):
        l_copy(k).wait_send()


def shards(lines, query, key_in, value, rates, residues, skip_gain, out_weight):
    rows, chans = query.shape
    groups = chans // GROUP
    subs = rows // SUB
    steps = (rows - SUB) // STEP
    half = chans // 2
    per_line = lax.axis_size("ctx") // lines
    own = MODES // per_line
    tile = chans // LANES
    hbm = pl.BlockSpec(memory_space=pl.ANY)
    vmem = pl.BlockSpec(memory_space=pltpu.VMEM)
    dma = pltpu.SemaphoreType.DMA
    return pl.pallas_call(
        functools.partial(kernel, lines),
        name="hyena",
        out_shape=pltpu.VMEM((rows, chans), BF16),
        in_specs=[hbm, hbm, hbm, hbm, vmem, vmem, vmem],
        out_specs=vmem,
        scratch_shapes=[
            pltpu.VMEM((rows, chans), BF16),
            pltpu.VMEM((rows, chans), BF16),
            pltpu.VMEM((rows, chans), BF16),
            pltpu.VMEM((rows, chans), BF16),
            pltpu.VMEM((4, chans, chans), BF16),
            pltpu.VMEM((rows, chans), BF16),
            pltpu.VMEM((rows, chans), F32),
            pltpu.VMEM((chans, 2 * SUB), BF16),
            pltpu.VMEM((SUB, chans), BF16),
            pltpu.VMEM((SUB, chans), BF16),
            pltpu.VMEM((groups, 2 * SUB), F32),
            pltpu.VMEM((groups // 2, SUB, 2 * SUB), BF16),
            pltpu.VMEM((subs, MODES, chans), F32),
            pltpu.VMEM((MODES, tile, LANES), F32),
            pltpu.VMEM((per_line, own, tile, LANES), F32),
            pltpu.VMEM((per_line, own, tile, LANES), F32),
            pltpu.VMEM((own, tile, LANES), F32),
            pltpu.VMEM((lines, own, tile, LANES), F32),
            pltpu.VMEM((per_line, own, tile, LANES), F32),
            pltpu.VMEM((per_line, own, tile, LANES), F32),
            pltpu.VMEM((2, SUB, half), BF16),
            pltpu.VMEM((2, SUB, half), BF16),
            pltpu.VMEM((2, 2, SUB, half), BF16),
            pltpu.VMEM((2, 2, SUB, half), BF16),
            pltpu.VMEM((2, chans, chans), BF16),
            pltpu.VMEM((steps, STEP, chans), BF16),
            pltpu.VMEM((steps, STEP, chans), BF16),
            pltpu.VMEM((steps, STEP, chans), BF16),
            dma((7,)),
            dma((per_line,)),
            dma((per_line,)),
            dma((lines,)),
            dma((lines,)),
            dma((per_line,)),
            dma((per_line,)),
            dma((2,)),
            dma((2,)),
            dma((2, 2)),
            dma((2, 2)),
            dma((4,)),
            dma((4,)),
            dma((4, 2)),
            dma((4, 2)),
            dma((4, 2)),
            dma((4, 2)),
            dma((2,)),
            dma((2,)),
            dma((steps,)),
            dma((steps,)),
            dma((steps,)),
            dma((steps,)),
        ],
        compiler_params=pltpu.CompilerParams(
            collective_id=0, has_side_effects=True, vmem_limit_bytes=56 * 1024 * 1024
        ),
    )(query, key_in, value, out_weight, rates.T, residues.T, skip_gain[None, :])


def solution(mesh):
    in_specs = (
        P("ctx", "tp"),
        P("ctx", "tp"),
        P("ctx", "tp"),
        P("tp", None),
        P("tp", None),
        P("tp"),
        P("tp", None),
    )
    lines = max(1, mesh.shape["ctx"] // MODES)
    return jax.shard_map(
        functools.partial(shards, lines),
        mesh=mesh,
        in_specs=in_specs,
        out_specs=P("ctx", "tp"),
        check_vma=False,
    )
```

```python
import functools

import jax
import jax.numpy as jnp
from jax import lax
from jax.experimental import pallas as pl
from jax.experimental.pallas import tpu as pltpu
from jax.sharding import PartitionSpec as P

GROUP = 16
MODES = 16
SUB = 128
LANES = 128
BLK = 256
STEP = 64
MESH = pl.DeviceIdType.MESH
F32 = jnp.float32
BF16 = jnp.bfloat16


def dot(a, b):
    return jnp.dot(a, b, preferred_element_type=F32)


def split(a):
    high = a.astype(BF16)
    return high, (a - high.astype(F32)).astype(BF16)


def kernel(
    lines,
    q_hbm,
    k_hbm,
    v_hbm,
    w_hbm,
    rates_ref,
    residues_ref,
    skip_ref,
    ob,
    qb,
    kb,
    vb,
    ub,
    wb,
    mixed,
    local,
    d_tab,
    a_hi,
    a_lo,
    h_pad,
    toep,
    sums,
    rate3,
    s_send,
    s_recv,
    l_send,
    l_recv,
    x_send,
    x_recv,
    far_s,
    far_r,
    near_s,
    near_r,
    wp,
    pair_r,
    sum_s,
    sum_r,
    lsem,
    s_ss,
    s_rs,
    l_ss,
    l_rs,
    x_ss,
    x_rs,
    far_ss,
    far_rs,
    near_ss,
    near_rs,
    wy_ss,
    wy_rs,
    wx_ss,
    wx_rs,
    wf_ss,
    wf_rs,
    sib_ss,
    sib_rs,
    pair_ss,
    pair_rs,
    sum_ss,
    sum_rs,
):
    rows, chans = ub.shape
    subs = rows // SUB
    groups = chans // GROUP
    blocks = chans // BLK
    half = chans // 2
    per_line = s_send.shape[0]
    own = s_send.shape[1]

    ctx, tp = lax.axis_index("ctx"), lax.axis_index("tp")
    mx, mj = lax.div(ctx, per_line), lax.rem(ctx, per_line)
    right, left = lax.rem(tp + 1, 4), lax.rem(tp + 3, 4)
    sides = ((ctx, right), (ctx, left))
    odd = lax.rem(tp, 2)
    pair, opp = tp + 1 - 2 * odd, 3 - tp
    way_pair, way_opp = odd, 1 - odd
    core = lax.rem(ctx, 2)
    sibling = ctx + 1 - 2 * core
    slice_rows, piece_rows = chans // 8, chans // 16
    pieces = 4
    step_rows = STEP
    steps = (rows - SUB) // step_rows

    order = sorted(range(1, per_line), key=lambda k: abs(2 * k - per_line))

    def peer_j(k):
        return lax.rem(mj + k, per_line)

    def peer_x(k):
        return lax.rem(mx + k, lines)

    barrier = pltpu.get_barrier_semaphore()
    for k in range(1, per_line):
        pl.semaphore_signal(
            barrier, inc=1, device_id=(mx * per_line + peer_j(k), tp), device_id_type=MESH
        )
    for k in range(1, lines):
        pl.semaphore_signal(
            barrier, inc=1, device_id=(peer_x(k) * per_line + mj, tp), device_id_type=MESH
        )
    for side in sides:
        pl.semaphore_signal(barrier, inc=1, device_id=side, device_id_type=MESH)

    loads = [
        pltpu.make_async_copy(k_hbm, kb, lsem.at[0]),
        pltpu.make_async_copy(v_hbm, vb, lsem.at[1]),
        pltpu.make_async_copy(q_hbm, qb, lsem.at[2]),
    ]
    w_loads = {}
    for r in (2, 1, 3, 0):
        start = pl.multiple_of(lax.rem(tp + r, 4) * chans, chans)
        w_loads[r] = pltpu.make_async_copy(
            w_hbm.at[:, pl.ds(start, chans)], wb.at[r], lsem.at[3 + r]
        )
    loads[0].start()
    loads[1].start()

    rates, residues = rates_ref[...].T, residues_ref[...].T
    pick = lax.broadcasted_iota(jnp.int32, (chans, MODES), 1) == (
        lax.broadcasted_iota(jnp.int32, (chans, MODES), 0) & (MODES - 1)
    )

    def column(a):
        spread = jnp.broadcast_to(a[:, None, :], (groups, MODES, MODES)).reshape(chans, MODES)
        return jnp.sum(jnp.where(pick, spread, 0.0), axis=1, keepdims=True)

    rate_col, residue_col = column(rates), column(residues)
    lag = lax.broadcasted_iota(jnp.int32, (chans, SUB), 1).astype(F32)
    decay_in = jnp.exp(-rate_col * (SUB - 1.0 - lag))
    high, low = split(decay_in)
    d_tab[:, :SUB] = high
    d_tab[:, SUB:] = low
    spread = (
        lax.shift_right_logical(lax.broadcasted_iota(jnp.int32, (groups, chans), 1), 4)
        == lax.broadcasted_iota(jnp.int32, (groups, chans), 0)
    ).astype(F32)
    rate_row = jnp.dot(
        rates_ref[...], spread, precision=lax.Precision.HIGHEST, preferred_element_type=F32
    )
    for k in range(chans // LANES):
        rate3[:, k, :] = rate_row[:, k * LANES : (k + 1) * LANES]
    same_group = lax.shift_right_logical(
        lax.broadcasted_iota(jnp.int32, (BLK, BLK), 0), 4
    ) == lax.shift_right_logical(lax.broadcasted_iota(jnp.int32, (BLK, BLK), 1), 4)
    diag = same_group.astype(F32)

    loads[0].wait()
    loads[1].wait()
    loads[2].start()
    for load in w_loads.values():
        load.start()
    for j in range(subs):
        at = pl.ds(j * SUB, SUB)
        for b in range(blocks):
            cols = pl.ds(b * BLK, BLK)
            u = (kb[at, cols].astype(F32) * vb[at, cols].astype(F32)).astype(BF16)
            ub[at, cols] = u
            full = dot(d_tab[cols, :], jnp.concatenate([u, u], axis=0))
            sums[j, :, cols] = jnp.sum((full * diag).reshape(BLK // MODES, MODES, BLK), axis=0)
    step_decay = jnp.exp(-rate_row * SUB)
    state = jnp.zeros_like(rate_row)
    for j in range(subs):
        following = step_decay * state + sums[j]
        sums[j] = state
        state = following
    for k in range(chans // LANES):
        piece = state[:, k * LANES : (k + 1) * LANES]
        s_send[:, :, k, :] = piece.reshape(per_line, own, LANES)

    pl.semaphore_wait(barrier, per_line - 1 + lines - 1 + 2)

    def s_copy(k):
        to = peer_j(k)
        return pltpu.make_async_remote_copy(
            src_ref=s_send.at[to],
            dst_ref=s_recv.at[mj],
            send_sem=s_ss.at[k],
            recv_sem=s_rs.at[k],
            device_id=(mx * per_line + to, tp),
            device_id_type=MESH,
        )

    def l_copy(k):
        return pltpu.make_async_remote_copy(
            src_ref=l_send,
            dst_ref=l_recv.at[mx],
            send_sem=l_ss.at[k],
            recv_sem=l_rs.at[k],
            device_id=(peer_x(k) * per_line + mj, tp),
            device_id_type=MESH,
        )

    def x_copy(k):
        to = peer_j(k)
        return pltpu.make_async_remote_copy(
            src_ref=x_send.at[to],
            dst_ref=x_recv.at[mj],
            send_sem=x_ss.at[k],
            recv_sem=x_rs.at[k],
            device_id=(mx * per_line + to, tp),
            device_id_type=MESH,
        )

    def piece(k, slot, lead, size):
        start = core * (chans // 2) + slot * slice_rows + (k % 2) * piece_rows + lead
        return pl.ds(pl.multiple_of(start, piece_rows // 2), size)

    def wy_copy(k):
        block = 1 - k // 2
        column = pair if block == 0 else 3 - pair
        at = piece(k, mx, 0, piece_rows)
        return pltpu.make_async_remote_copy(
            src_ref=w_hbm.at[at, pl.ds(pl.multiple_of(column * chans, chans), chans)],
            dst_ref=wp.at[block, at],
            send_sem=wy_ss.at[k],
            recv_sem=wy_rs.at[k],
            device_id=(ctx, pair),
            device_id_type=MESH,
        )

    def x_side(way):
        return (peer_x(1 if way == 0 else lines - 1) * per_line + mj, tp)

    def wx_copy(k, way):
        ref = wp.at[1 - k // 2, piece(k, mx, 0, piece_rows)]
        return pltpu.make_async_remote_copy(
            src_ref=ref,
            dst_ref=ref,
            send_sem=wx_ss.at[k, way],
            recv_sem=wx_rs.at[k, way],
            device_id=x_side(way),
            device_id_type=MESH,
        )

    def wf_copy(k, way):
        slot = peer_x(lines - 1 if way == 0 else 1)
        ref = wp.at[1 - k // 2, piece(k, slot, way * (piece_rows // 2), piece_rows // 2)]
        return pltpu.make_async_remote_copy(
            src_ref=ref,
            dst_ref=ref,
            send_sem=wf_ss.at[k, way],
            recv_sem=wf_rs.at[k, way],
            device_id=x_side(way),
            device_id_type=MESH,
        )

    def sib_copy(block):
        ref = wp.at[block, pl.ds(pl.multiple_of(core * (chans // 2), chans // 2), chans // 2)]
        return pltpu.make_async_remote_copy(
            src_ref=ref,
            dst_ref=ref,
            send_sem=sib_ss.at[block],
            recv_sem=sib_rs.at[block],
            device_id=(sibling, tp),
            device_id_type=MESH,
        )

    def spread_piece(k):
        wy_copy(k).wait_recv()
        for way in range(2):
            wx_copy(k, way).start()

    def pass_piece(k):
        for way in range(2):
            wx_copy(k, way).wait_recv()
            wf_copy(k, way).start()

    def share_block(block):
        for k in (2 - 2 * block, 3 - 2 * block):
            for way in range(2):
                wf_copy(k, way).wait_recv()
        sib_copy(block).start()

    for k in order:
        s_copy(k).start()
    for k in range(pieces):
        wy_copy(k).start()
    s_recv[mj] = s_send[mj]

    taps = jnp.sum((decay_in * residue_col).reshape(groups, MODES, SUB), axis=1)
    h_pad[:, :SUB] = taps
    h_pad[:, SUB:] = jnp.zeros_like(taps)

    def build(n, carry):
        for side in range(2):
            row = jnp.broadcast_to(h_pad[pl.ds(2 * n + side, 1), :], (SUB, 2 * SUB))
            turned = pltpu.roll(row, SUB + 1, 1, stride=1, stride_axis=0)
            toep[n, :, side * SUB : (side + 1) * SUB] = turned[:, :SUB].astype(BF16)
        return carry

    lax.fori_loop(0, groups // 2, build, 0)

    my_rate = rate3[pl.ds(mj * own, own)]
    block_decay = jnp.exp(-my_rate * rows)
    weights = []
    for other in range(lines):
        distance = mx - 1 - other
        span = jnp.maximum(distance, 0) * (per_line * rows)
        weights.append(jnp.where(distance >= 0, jnp.exp(-my_rate * span.astype(F32)), 0.0))
    for k in range(1, per_line):
        s_copy(k).wait_recv()
    total = jnp.zeros_like(my_rate)
    for j in range(per_line):
        x_send[j] = total
        total = block_decay * total + s_recv[j]
    l_send[...] = total
    l_recv[mx] = total
    for k in range(1, lines):
        l_copy(k).start()
    spread_piece(0)

    def inside(n, carry):
        j, b = lax.div(n, blocks), lax.rem(n, blocks)
        at = pl.ds(pl.multiple_of(j * SUB, SUB), SUB)
        cols = pl.ds(pl.multiple_of(b * BLK, BLK), BLK)
        u = ub[at, cols]
        acc = skip_ref[:, cols] * u.astype(F32)
        lane_group = lax.shift_right_logical(lax.broadcasted_iota(jnp.int32, (1, BLK), 1), 4)
        for pair in range(BLK // GROUP // 2):
            masked = [
                u * (lane_group == 2 * pair + side).astype(F32).astype(BF16) for side in range(2)
            ]
            acc += dot(toep[b * (BLK // GROUP // 2) + pair], jnp.concatenate(masked, axis=0))
        local[at, cols] = acc
        return carry

    first_part = subs * blocks // 2
    lax.fori_loop(0, first_part, inside, 0)
    spread_piece(1)

    for k in range(1, lines):
        l_copy(k).wait_recv()
    entering = jnp.zeros_like(total)
    for other in range(lines):
        entering += weights[other] * l_recv[other]
    for j in range(per_line):
        x_send[j] = x_send[j] + entering
        entering = entering * block_decay
    for k in order:
        x_copy(k).start()
    x_recv[mj] = x_send[mj]

    high, low = split((residue_col * jnp.exp(-rate_col * (lag + 1.0))).T)
    a_hi[...] = high
    a_lo[...] = low
    lax.fori_loop(first_part, subs * blocks, inside, 0)
    pass_piece(0)
    spread_piece(2)
    pass_piece(1)
    loads[2].wait()
    for k in range(1, per_line):
        x_copy(k).wait_recv()

    def side_of(way):
        return (ctx, lax.rem(tp + 1 + 2 * way, 4))

    def far_copy(way):
        return pltpu.make_async_remote_copy(
            src_ref=far_s.at[way],
            dst_ref=far_r.at[way],
            send_sem=far_ss.at[way],
            recv_sem=far_rs.at[way],
            device_id=side_of(way),
            device_id_type=MESH,
        )

    def near_copy(way, part):
        return pltpu.make_async_remote_copy(
            src_ref=near_s.at[way, part],
            dst_ref=near_r.at[way, part],
            send_sem=near_ss.at[way, part],
            recv_sem=near_rs.at[way, part],
            device_id=side_of(way),
            device_id_type=MESH,
        )

    def tokens(h, skip=SUB, size=step_rows):
        return pl.ds(pl.multiple_of(skip + h * size, step_rows), size)

    def pair_copy(h):
        return pltpu.make_async_remote_copy(
            src_ref=mixed.at[tokens(h)],
            dst_ref=pair_r.at[tokens(h, 0)],
            send_sem=pair_ss.at[h],
            recv_sem=pair_rs.at[h],
            device_id=(ctx, pair),
            device_id_type=MESH,
        )

    def sum_copy(h):
        return pltpu.make_async_remote_copy(
            src_ref=sum_s.at[tokens(h, 0)],
            dst_ref=sum_r.at[tokens(h, 0)],
            send_sem=sum_ss.at[h],
            recv_sem=sum_rs.at[h],
            device_id=(ctx, opp),
            device_id_type=MESH,
        )

    def project(r, part):
        cols = pl.ds(pl.multiple_of(part * half, half), half)
        return dot(mixed[:SUB, :], wb[r, :, cols])

    w_loads[2].wait()
    entry = jnp.concatenate(
        [x_recv[:, :, k, :].reshape(MODES, LANES) for k in range(chans // LANES)], axis=1
    )
    diag_bf = diag.astype(BF16)

    def mix(j):
        at = pl.ds(pl.multiple_of(j * SUB, SUB), SUB)
        start = jnp.exp(-rate_row * (j * SUB * 1.0)) * entry + sums[j]
        x_hi, x_lo = split(start)
        for b in range(blocks):
            cols = slice(b * BLK, (b + 1) * BLK)
            wide_hi = jnp.concatenate([x_hi[:, cols]] * (BLK // MODES), axis=0) * diag_bf
            wide_lo = jnp.concatenate([x_lo[:, cols]] * (BLK // MODES), axis=0) * diag_bf
            past = dot(a_hi[:, cols], wide_hi) + dot(a_lo[:, cols], wide_hi)
            past += dot(a_hi[:, cols], wide_lo)
            mixed[at, cols] = (qb[at, cols].astype(F32) * (local[at, cols] + past)).astype(BF16)

    per_sub = SUB // step_rows

    def mix_and_send(j):
        mix(j)
        for h in range((j - 1) * per_sub, j * per_sub):
            pair_copy(h).start()

    def direct(way):
        near_s[way, 1 - way] = project(1 + 2 * way, 1 - way).astype(BF16)
        near_copy(way, 1 - way).start()

    def joint(way):
        part = project(1 + 2 * way, way)
        far_copy(way).wait_recv()
        near_s[way, way] = (part + far_r[way].astype(F32)).astype(BF16)
        near_copy(way, way).start()

    mix(0)
    for way in range(2):
        far_s[way] = project(2, way).astype(BF16)
        far_copy(way).start()
    mix_and_send(1)
    w_loads[1].wait()
    w_loads[3].wait()
    direct(way_opp)
    for j in range(2, subs):
        mix_and_send(j)
    spread_piece(3)
    joint(way_opp)
    share_block(1)
    direct(way_pair)
    joint(way_pair)
    pass_piece(2)
    w_loads[0].wait()
    for part in range(2):
        cols = slice(part * half, (part + 1) * half)
        local[:SUB, cols] = project(0, part)

    opp_slot = 3 - 2 * odd

    def sum_step(h):
        pair_copy(h).wait_recv()
        mine, theirs = mixed[tokens(h), :], pair_r[tokens(h, 0), :]
        for part in range(2):
            cols = slice(part * half, (part + 1) * half)
            both = dot(mine, wb[opp_slot, :, cols]) + dot(theirs, wp[1, :, cols])
            sum_s[tokens(h, 0), cols] = both.astype(BF16)
        sum_copy(h).start()

    def own_step(n):
        at, off = tokens(n, SUB, SUB), tokens(n, 0, SUB)
        mine, theirs = mixed[at, :], pair_r[off, :]
        for part in range(2):
            cols = slice(part * half, (part + 1) * half)
            local[at, cols] = dot(mine, wb[0, :, cols]) + dot(theirs, wp[0, :, cols])

    def finish(n):
        for h in range(n * per_sub, (n + 1) * per_sub):
            sum_copy(h).wait_recv()
            ob[tokens(h), :] = (local[tokens(h), :] + sum_r[tokens(h, 0), :].astype(F32)).astype(BF16)

    sib_copy(1).wait_recv()
    sum_step(0)
    pass_piece(3)
    sum_step(1)
    share_block(0)
    sum_step(2)
    sum_step(3)
    sib_copy(0).wait_recv()
    own_step(0)
    sum_step(4)
    sum_step(5)
    finish(0)
    own_step(1)
    own_step(2)
    finish(1)
    finish(2)
    for part in range(2):
        cols = slice(part * half, (part + 1) * half)
        near_copy(0, part).wait_recv()
        near_copy(1, part).wait_recv()
        total = local[:SUB, cols] + near_r[0, part].astype(F32) + near_r[1, part].astype(F32)
        ob[:SUB, cols] = total.astype(BF16)

    for way in range(2):
        far_copy(way).wait_send()
        for part in range(2):
            near_copy(way, part).wait_send()
        for k in range(pieces):
            wx_copy(k, way).wait_send()
            wf_copy(k, way).wait_send()
        sib_copy(way).wait_send()
    for k in range(pieces):
        wy_copy(k).wait_send()
    for h in range(steps):
        pair_copy(h).wait_send()
        sum_copy(h).wait_send()
    for k in range(1, per_line):
        s_copy(k).wait_send()
        x_copy(k).wait_send()
    for k in range(1, lines):
        l_copy(k).wait_send()


def shards(lines, query, key_in, value, rates, residues, skip_gain, out_weight):
    rows, chans = query.shape
    groups = chans // GROUP
    subs = rows // SUB
    steps = (rows - SUB) // STEP
    half = chans // 2
    per_line = lax.axis_size("ctx") // lines
    own = MODES // per_line
    tile = chans // LANES
    hbm = pl.BlockSpec(memory_space=pl.ANY)
    vmem = pl.BlockSpec(memory_space=pltpu.VMEM)
    dma = pltpu.SemaphoreType.DMA
    return pl.pallas_call(
        functools.partial(kernel, lines),
        name="hyena",
        out_shape=pltpu.VMEM((rows, chans), BF16),
        in_specs=[hbm, hbm, hbm, hbm, vmem, vmem, vmem],
        out_specs=vmem,
        scratch_shapes=[
            pltpu.VMEM((rows, chans), BF16),
            pltpu.VMEM((rows, chans), BF16),
            pltpu.VMEM((rows, chans), BF16),
            pltpu.VMEM((rows, chans), BF16),
            pltpu.VMEM((4, chans, chans), BF16),
            pltpu.VMEM((rows, chans), BF16),
            pltpu.VMEM((rows, chans), F32),
            pltpu.VMEM((chans, 2 * SUB), BF16),
            pltpu.VMEM((SUB, chans), BF16),
            pltpu.VMEM((SUB, chans), BF16),
            pltpu.VMEM((groups, 2 * SUB), F32),
            pltpu.VMEM((groups // 2, SUB, 2 * SUB), BF16),
            pltpu.VMEM((subs, MODES, chans), F32),
            pltpu.VMEM((MODES, tile, LANES), F32),
            pltpu.VMEM((per_line, own, tile, LANES), F32),
            pltpu.VMEM((per_line, own, tile, LANES), F32),
            pltpu.VMEM((own, tile, LANES), F32),
            pltpu.VMEM((lines, own, tile, LANES), F32),
            pltpu.VMEM((per_line, own, tile, LANES), F32),
            pltpu.VMEM((per_line, own, tile, LANES), F32),
            pltpu.VMEM((2, SUB, half), BF16),
            pltpu.VMEM((2, SUB, half), BF16),
            pltpu.VMEM((2, 2, SUB, half), BF16),
            pltpu.VMEM((2, 2, SUB, half), BF16),
            pltpu.VMEM((2, chans, chans), BF16),
            pltpu.VMEM((rows - SUB, chans), BF16),
            pltpu.VMEM((rows - SUB, chans), BF16),
            pltpu.VMEM((rows - SUB, chans), BF16),
            dma((7,)),
            dma((per_line,)),
            dma((per_line,)),
            dma((lines,)),
            dma((lines,)),
            dma((per_line,)),
            dma((per_line,)),
            dma((2,)),
            dma((2,)),
            dma((2, 2)),
            dma((2, 2)),
            dma((4,)),
            dma((4,)),
            dma((4, 2)),
            dma((4, 2)),
            dma((4, 2)),
            dma((4, 2)),
            dma((2,)),
            dma((2,)),
            dma((steps,)),
            dma((steps,)),
            dma((steps,)),
            dma((steps,)),
        ],
        compiler_params=pltpu.CompilerParams(
            collective_id=0, has_side_effects=True, vmem_limit_bytes=56 * 1024 * 1024
        ),
    )(query, key_in, value, out_weight, rates.T, residues.T, skip_gain[None, :])


def solution(mesh):
    in_specs = (
        P("ctx", "tp"),
        P("ctx", "tp"),
        P("ctx", "tp"),
        P("tp", None),
        P("tp", None),
        P("tp"),
        P("tp", None),
    )
    lines = max(1, mesh.shape["ctx"] // MODES)
    return jax.shard_map(
        functools.partial(shards, lines),
        mesh=mesh,
        in_specs=in_specs,
        out_specs=P("ctx", "tp"),
        check_vma=False,
    )
```

```python
import functools

import jax
import jax.numpy as jnp
from jax import lax
from jax.experimental import pallas as pl
from jax.experimental.pallas import tpu as pltpu
from jax.sharding import PartitionSpec as P

GROUP = 16
MODES = 16
SUB = 128
LANES = 128
BLK = 256
STEP = 64
MESH = pl.DeviceIdType.MESH
F32 = jnp.float32
BF16 = jnp.bfloat16


def dot(a, b):
    return jnp.dot(a, b, preferred_element_type=F32)


def split(a):
    high = a.astype(BF16)
    return high, (a - high.astype(F32)).astype(BF16)


def kernel(
    lines,
    q_hbm,
    k_hbm,
    v_hbm,
    w_hbm,
    rates_ref,
    residues_ref,
    skip_ref,
    ob,
    qb,
    kb,
    vb,
    ub,
    wb,
    mixed,
    local,
    d_tab,
    a_hi,
    a_lo,
    h_pad,
    toep,
    sums,
    rate3,
    s_send,
    s_recv,
    l_send,
    l_recv,
    x_send,
    x_recv,
    far_s,
    far_r,
    near_s,
    near_r,
    wp,
    pair_r,
    sum_s,
    sum_r,
    lsem,
    s_ss,
    s_rs,
    l_ss,
    l_rs,
    x_ss,
    x_rs,
    far_ss,
    far_rs,
    near_ss,
    near_rs,
    wy_ss,
    wy_rs,
    wx_ss,
    wx_rs,
    wf_ss,
    wf_rs,
    sib_ss,
    sib_rs,
    pair_ss,
    pair_rs,
    sum_ss,
    sum_rs,
):
    rows, chans = ub.shape
    subs = rows // SUB
    groups = chans // GROUP
    blocks = chans // BLK
    half = chans // 2
    per_line = s_send.shape[0]
    own = s_send.shape[1]

    ctx, tp = lax.axis_index("ctx"), lax.axis_index("tp")
    mx, mj = lax.div(ctx, per_line), lax.rem(ctx, per_line)
    right, left = lax.rem(tp + 1, 4), lax.rem(tp + 3, 4)
    sides = ((ctx, right), (ctx, left))
    odd = lax.rem(tp, 2)
    pair, opp = tp + 1 - 2 * odd, 3 - tp
    way_pair, way_opp = odd, 1 - odd
    core = lax.rem(ctx, 2)
    sibling = ctx + 1 - 2 * core
    piece_rows = chans // 16
    pieces = 4
    step_rows = STEP
    steps = (rows - SUB) // step_rows

    order = sorted(range(1, per_line), key=lambda k: abs(2 * k - per_line))

    def peer_j(k):
        return lax.rem(mj + k, per_line)

    def peer_x(k):
        return lax.rem(mx + k, lines)

    barrier = pltpu.get_barrier_semaphore()
    for k in range(1, per_line):
        pl.semaphore_signal(
            barrier, inc=1, device_id=(mx * per_line + peer_j(k), tp), device_id_type=MESH
        )
    for k in range(1, lines):
        pl.semaphore_signal(
            barrier, inc=1, device_id=(peer_x(k) * per_line + mj, tp), device_id_type=MESH
        )
    for side in sides:
        pl.semaphore_signal(barrier, inc=1, device_id=side, device_id_type=MESH)

    loads = [
        pltpu.make_async_copy(k_hbm, kb, lsem.at[0]),
        pltpu.make_async_copy(v_hbm, vb, lsem.at[1]),
        pltpu.make_async_copy(q_hbm, qb, lsem.at[2]),
    ]
    w_loads = {}
    for r in (2, 1, 3, 0):
        start = pl.multiple_of(lax.rem(tp + r, 4) * chans, chans)
        w_loads[r] = pltpu.make_async_copy(
            w_hbm.at[:, pl.ds(start, chans)], wb.at[r], lsem.at[3 + r]
        )
    loads[0].start()
    loads[1].start()

    rates, residues = rates_ref[...].T, residues_ref[...].T
    pick = lax.broadcasted_iota(jnp.int32, (chans, MODES), 1) == (
        lax.broadcasted_iota(jnp.int32, (chans, MODES), 0) & (MODES - 1)
    )

    def column(a):
        spread = jnp.broadcast_to(a[:, None, :], (groups, MODES, MODES)).reshape(chans, MODES)
        return jnp.sum(jnp.where(pick, spread, 0.0), axis=1, keepdims=True)

    rate_col, residue_col = column(rates), column(residues)
    lag = lax.broadcasted_iota(jnp.int32, (chans, SUB), 1).astype(F32)
    decay_in = jnp.exp(-rate_col * (SUB - 1.0 - lag))
    high, low = split(decay_in)
    d_tab[:, :SUB] = high
    d_tab[:, SUB:] = low
    spread = (
        lax.shift_right_logical(lax.broadcasted_iota(jnp.int32, (groups, chans), 1), 4)
        == lax.broadcasted_iota(jnp.int32, (groups, chans), 0)
    ).astype(F32)
    rate_row = jnp.dot(
        rates_ref[...], spread, precision=lax.Precision.HIGHEST, preferred_element_type=F32
    )
    for k in range(chans // LANES):
        rate3[:, k, :] = rate_row[:, k * LANES : (k + 1) * LANES]
    same_group = lax.shift_right_logical(
        lax.broadcasted_iota(jnp.int32, (BLK, BLK), 0), 4
    ) == lax.shift_right_logical(lax.broadcasted_iota(jnp.int32, (BLK, BLK), 1), 4)
    diag = same_group.astype(F32)

    loads[0].wait()
    loads[1].wait()
    loads[2].start()
    for load in w_loads.values():
        load.start()
    for j in range(subs):
        at = pl.ds(j * SUB, SUB)
        for b in range(blocks):
            cols = pl.ds(b * BLK, BLK)
            u = (kb[at, cols].astype(F32) * vb[at, cols].astype(F32)).astype(BF16)
            ub[at, cols] = u
            full = dot(d_tab[cols, :], jnp.concatenate([u, u], axis=0))
            sums[j, :, cols] = jnp.sum((full * diag).reshape(BLK // MODES, MODES, BLK), axis=0)
    step_decay = jnp.exp(-rate_row * SUB)
    state = jnp.zeros_like(rate_row)
    for j in range(subs):
        following = step_decay * state + sums[j]
        sums[j] = state
        state = following
    for k in range(chans // LANES):
        piece = state[:, k * LANES : (k + 1) * LANES]
        s_send[:, :, k, :] = piece.reshape(per_line, own, LANES)

    pl.semaphore_wait(barrier, per_line - 1 + lines - 1 + 2)

    def s_copy(k):
        to = peer_j(k)
        return pltpu.make_async_remote_copy(
            src_ref=s_send.at[to],
            dst_ref=s_recv.at[mj],
            send_sem=s_ss.at[k],
            recv_sem=s_rs.at[k],
            device_id=(mx * per_line + to, tp),
            device_id_type=MESH,
        )

    def l_copy(k):
        return pltpu.make_async_remote_copy(
            src_ref=l_send,
            dst_ref=l_recv.at[mx],
            send_sem=l_ss.at[k],
            recv_sem=l_rs.at[k],
            device_id=(peer_x(k) * per_line + mj, tp),
            device_id_type=MESH,
        )

    def x_copy(k):
        to = peer_j(k)
        return pltpu.make_async_remote_copy(
            src_ref=x_send.at[to],
            dst_ref=x_recv.at[mj],
            send_sem=x_ss.at[k],
            recv_sem=x_rs.at[k],
            device_id=(mx * per_line + to, tp),
            device_id_type=MESH,
        )

    def piece(k, slot, lead, size):
        start = core * (chans // 2) + (k % 2) * (chans // 4) + slot * piece_rows + lead
        return pl.ds(pl.multiple_of(start, piece_rows // 2), size)

    def wy_copy(k):
        block = 1 - k // 2
        column = pair if block == 0 else 3 - pair
        at = piece(k, mx, 0, piece_rows)
        return pltpu.make_async_remote_copy(
            src_ref=w_hbm.at[at, pl.ds(pl.multiple_of(column * chans, chans), chans)],
            dst_ref=wp.at[block, at],
            send_sem=wy_ss.at[k],
            recv_sem=wy_rs.at[k],
            device_id=(ctx, pair),
            device_id_type=MESH,
        )

    def x_side(way):
        return (peer_x(1 if way == 0 else lines - 1) * per_line + mj, tp)

    def wx_copy(k, way):
        ref = wp.at[1 - k // 2, piece(k, mx, 0, piece_rows)]
        return pltpu.make_async_remote_copy(
            src_ref=ref,
            dst_ref=ref,
            send_sem=wx_ss.at[k, way],
            recv_sem=wx_rs.at[k, way],
            device_id=x_side(way),
            device_id_type=MESH,
        )

    def wf_copy(k, way):
        slot = peer_x(lines - 1 if way == 0 else 1)
        ref = wp.at[1 - k // 2, piece(k, slot, way * (piece_rows // 2), piece_rows // 2)]
        return pltpu.make_async_remote_copy(
            src_ref=ref,
            dst_ref=ref,
            send_sem=wf_ss.at[k, way],
            recv_sem=wf_rs.at[k, way],
            device_id=x_side(way),
            device_id_type=MESH,
        )

    def sib_copy(k):
        start = core * (chans // 2) + (k % 2) * (chans // 4)
        ref = wp.at[1 - k // 2, pl.ds(pl.multiple_of(start, chans // 4), chans // 4)]
        return pltpu.make_async_remote_copy(
            src_ref=ref,
            dst_ref=ref,
            send_sem=sib_ss.at[k],
            recv_sem=sib_rs.at[k],
            device_id=(sibling, tp),
            device_id_type=MESH,
        )

    def spread_piece(k):
        wy_copy(k).wait_recv()
        for way in range(2):
            wx_copy(k, way).start()

    def pass_piece(k):
        for way in range(2):
            wx_copy(k, way).wait_recv()
            wf_copy(k, way).start()

    def share_piece(k):
        for way in range(2):
            wf_copy(k, way).wait_recv()
        sib_copy(k).start()

    for k in order:
        s_copy(k).start()
    for k in range(pieces):
        wy_copy(k).start()
    s_recv[mj] = s_send[mj]

    taps = jnp.sum((decay_in * residue_col).reshape(groups, MODES, SUB), axis=1)
    h_pad[:, :SUB] = taps
    h_pad[:, SUB:] = jnp.zeros_like(taps)

    def build(n, carry):
        for side in range(2):
            row = jnp.broadcast_to(h_pad[pl.ds(2 * n + side, 1), :], (SUB, 2 * SUB))
            turned = pltpu.roll(row, SUB + 1, 1, stride=1, stride_axis=0)
            toep[n, :, side * SUB : (side + 1) * SUB] = turned[:, :SUB].astype(BF16)
        return carry

    lax.fori_loop(0, groups // 2, build, 0)

    my_rate = rate3[pl.ds(mj * own, own)]
    block_decay = jnp.exp(-my_rate * rows)
    weights = []
    for other in range(lines):
        distance = mx - 1 - other
        span = jnp.maximum(distance, 0) * (per_line * rows)
        weights.append(jnp.where(distance >= 0, jnp.exp(-my_rate * span.astype(F32)), 0.0))
    for k in range(1, per_line):
        s_copy(k).wait_recv()
    total = jnp.zeros_like(my_rate)
    for j in range(per_line):
        x_send[j] = total
        total = block_decay * total + s_recv[j]
    l_send[...] = total
    l_recv[mx] = total
    for k in range(1, lines):
        l_copy(k).start()
    spread_piece(0)

    def inside(n, carry):
        j, b = lax.div(n, blocks), lax.rem(n, blocks)
        at = pl.ds(pl.multiple_of(j * SUB, SUB), SUB)
        cols = pl.ds(pl.multiple_of(b * BLK, BLK), BLK)
        u = ub[at, cols]
        acc = skip_ref[:, cols] * u.astype(F32)
        lane_group = lax.shift_right_logical(lax.broadcasted_iota(jnp.int32, (1, BLK), 1), 4)
        for pair in range(BLK // GROUP // 2):
            masked = [
                u * (lane_group == 2 * pair + side).astype(F32).astype(BF16) for side in range(2)
            ]
            acc += dot(toep[b * (BLK // GROUP // 2) + pair], jnp.concatenate(masked, axis=0))
        local[at, cols] = acc
        return carry

    first_part = subs * blocks // 2
    lax.fori_loop(0, first_part, inside, 0)
    spread_piece(1)

    for k in range(1, lines):
        l_copy(k).wait_recv()
    entering = jnp.zeros_like(total)
    for other in range(lines):
        entering += weights[other] * l_recv[other]
    for j in range(per_line):
        x_send[j] = x_send[j] + entering
        entering = entering * block_decay
    for k in order:
        x_copy(k).start()
    x_recv[mj] = x_send[mj]

    high, low = split((residue_col * jnp.exp(-rate_col * (lag + 1.0))).T)
    a_hi[...] = high
    a_lo[...] = low
    lax.fori_loop(first_part, subs * blocks, inside, 0)
    pass_piece(0)
    spread_piece(2)
    pass_piece(1)
    loads[2].wait()
    for k in range(1, per_line):
        x_copy(k).wait_recv()

    def side_of(way):
        return (ctx, lax.rem(tp + 1 + 2 * way, 4))

    def far_copy(way):
        return pltpu.make_async_remote_copy(
            src_ref=far_s.at[way],
            dst_ref=far_r.at[way],
            send_sem=far_ss.at[way],
            recv_sem=far_rs.at[way],
            device_id=side_of(way),
            device_id_type=MESH,
        )

    def near_copy(way, part):
        return pltpu.make_async_remote_copy(
            src_ref=near_s.at[way, part],
            dst_ref=near_r.at[way, part],
            send_sem=near_ss.at[way, part],
            recv_sem=near_rs.at[way, part],
            device_id=side_of(way),
            device_id_type=MESH,
        )

    def tokens(h, skip=SUB, size=step_rows):
        return pl.ds(pl.multiple_of(skip + h * size, step_rows), size)

    def pair_copy(h):
        return pltpu.make_async_remote_copy(
            src_ref=mixed.at[tokens(h)],
            dst_ref=pair_r.at[tokens(h, 0)],
            send_sem=pair_ss.at[h],
            recv_sem=pair_rs.at[h],
            device_id=(ctx, pair),
            device_id_type=MESH,
        )

    def sum_copy(h):
        return pltpu.make_async_remote_copy(
            src_ref=sum_s.at[tokens(h, 0)],
            dst_ref=sum_r.at[tokens(h, 0)],
            send_sem=sum_ss.at[h],
            recv_sem=sum_rs.at[h],
            device_id=(ctx, opp),
            device_id_type=MESH,
        )

    def project(r, part):
        cols = pl.ds(pl.multiple_of(part * half, half), half)
        return dot(mixed[:SUB, :], wb[r, :, cols])

    w_loads[2].wait()
    entry = jnp.concatenate(
        [x_recv[:, :, k, :].reshape(MODES, LANES) for k in range(chans // LANES)], axis=1
    )
    diag_bf = diag.astype(BF16)

    def mix(j):
        at = pl.ds(pl.multiple_of(j * SUB, SUB), SUB)
        start = jnp.exp(-rate_row * (j * SUB * 1.0)) * entry + sums[j]
        x_hi, x_lo = split(start)
        for b in range(blocks):
            cols = slice(b * BLK, (b + 1) * BLK)
            wide_hi = jnp.concatenate([x_hi[:, cols]] * (BLK // MODES), axis=0) * diag_bf
            wide_lo = jnp.concatenate([x_lo[:, cols]] * (BLK // MODES), axis=0) * diag_bf
            past = dot(a_hi[:, cols], wide_hi) + dot(a_lo[:, cols], wide_hi)
            past += dot(a_hi[:, cols], wide_lo)
            mixed[at, cols] = (qb[at, cols].astype(F32) * (local[at, cols] + past)).astype(BF16)

    per_sub = SUB // step_rows

    def mix_and_send(j):
        mix(j)
        for h in range((j - 1) * per_sub, j * per_sub):
            pair_copy(h).start()

    def direct(way):
        near_s[way, 1 - way] = project(1 + 2 * way, 1 - way).astype(BF16)
        near_copy(way, 1 - way).start()

    def joint(way):
        part = project(1 + 2 * way, way)
        far_copy(way).wait_recv()
        near_s[way, way] = (part + far_r[way].astype(F32)).astype(BF16)
        near_copy(way, way).start()

    def far(way):
        far_s[way] = project(2, way).astype(BF16)
        far_copy(way).start()

    mix(0)
    far(way_pair)
    far(way_opp)
    mix_and_send(1)
    w_loads[1].wait()
    w_loads[3].wait()
    direct(way_opp)
    share_piece(0)
    for j in range(2, subs):
        mix_and_send(j)
    spread_piece(3)
    joint(way_opp)
    share_piece(1)
    direct(way_pair)
    joint(way_pair)
    pass_piece(2)
    w_loads[0].wait()
    for part in range(2):
        cols = slice(part * half, (part + 1) * half)
        local[:SUB, cols] = project(0, part)

    opp_slot = 3 - 2 * odd

    def sum_step(h):
        pair_copy(h).wait_recv()
        mine, theirs = mixed[tokens(h), :], pair_r[tokens(h, 0), :]
        for part in range(2):
            cols = slice(part * half, (part + 1) * half)
            both = dot(mine, wb[opp_slot, :, cols]) + dot(theirs, wp[1, :, cols])
            sum_s[tokens(h, 0), cols] = both.astype(BF16)
        sum_copy(h).start()

    def own_step(n):
        at, off = tokens(n, SUB, SUB), tokens(n, 0, SUB)
        mine, theirs = mixed[at, :], pair_r[off, :]
        for part in range(2):
            cols = slice(part * half, (part + 1) * half)
            local[at, cols] = dot(mine, wb[0, :, cols]) + dot(theirs, wp[0, :, cols])

    def finish(n):
        for h in range(n * per_sub, (n + 1) * per_sub):
            sum_copy(h).wait_recv()
            ob[tokens(h), :] = (local[tokens(h), :] + sum_r[tokens(h, 0), :].astype(F32)).astype(BF16)

    sib_copy(0).wait_recv()
    sib_copy(1).wait_recv()
    sum_step(0)
    pass_piece(3)
    share_piece(2)
    sum_step(1)
    share_piece(3)
    sum_step(2)
    sum_step(3)
    sib_copy(2).wait_recv()
    sib_copy(3).wait_recv()
    own_step(0)
    sum_step(4)
    sum_step(5)
    finish(0)
    own_step(1)
    own_step(2)
    finish(1)
    finish(2)
    for part in range(2):
        cols = slice(part * half, (part + 1) * half)
        near_copy(0, part).wait_recv()
        near_copy(1, part).wait_recv()
        total = local[:SUB, cols] + near_r[0, part].astype(F32) + near_r[1, part].astype(F32)
        ob[:SUB, cols] = total.astype(BF16)

    for way in range(2):
        far_copy(way).wait_send()
        for part in range(2):
            near_copy(way, part).wait_send()
        for k in range(pieces):
            wx_copy(k, way).wait_send()
            wf_copy(k, way).wait_send()
    for k in range(pieces):
        wy_copy(k).wait_send()
        sib_copy(k).wait_send()
    for h in range(steps):
        pair_copy(h).wait_send()
        sum_copy(h).wait_send()
    for k in range(1, per_line):
        s_copy(k).wait_send()
        x_copy(k).wait_send()
    for k in range(1, lines):
        l_copy(k).wait_send()


def shards(lines, query, key_in, value, rates, residues, skip_gain, out_weight):
    rows, chans = query.shape
    groups = chans // GROUP
    subs = rows // SUB
    steps = (rows - SUB) // STEP
    half = chans // 2
    per_line = lax.axis_size("ctx") // lines
    own = MODES // per_line
    tile = chans // LANES
    hbm = pl.BlockSpec(memory_space=pl.ANY)
    vmem = pl.BlockSpec(memory_space=pltpu.VMEM)
    dma = pltpu.SemaphoreType.DMA
    return pl.pallas_call(
        functools.partial(kernel, lines),
        name="hyena",
        out_shape=pltpu.VMEM((rows, chans), BF16),
        in_specs=[hbm, hbm, hbm, hbm, vmem, vmem, vmem],
        out_specs=vmem,
        scratch_shapes=[
            pltpu.VMEM((rows, chans), BF16),
            pltpu.VMEM((rows, chans), BF16),
            pltpu.VMEM((rows, chans), BF16),
            pltpu.VMEM((rows, chans), BF16),
            pltpu.VMEM((4, chans, chans), BF16),
            pltpu.VMEM((rows, chans), BF16),
            pltpu.VMEM((rows, chans), F32),
            pltpu.VMEM((chans, 2 * SUB), BF16),
            pltpu.VMEM((SUB, chans), BF16),
            pltpu.VMEM((SUB, chans), BF16),
            pltpu.VMEM((groups, 2 * SUB), F32),
            pltpu.VMEM((groups // 2, SUB, 2 * SUB), BF16),
            pltpu.VMEM((subs, MODES, chans), F32),
            pltpu.VMEM((MODES, tile, LANES), F32),
            pltpu.VMEM((per_line, own, tile, LANES), F32),
            pltpu.VMEM((per_line, own, tile, LANES), F32),
            pltpu.VMEM((own, tile, LANES), F32),
            pltpu.VMEM((lines, own, tile, LANES), F32),
            pltpu.VMEM((per_line, own, tile, LANES), F32),
            pltpu.VMEM((per_line, own, tile, LANES), F32),
            pltpu.VMEM((2, SUB, half), BF16),
            pltpu.VMEM((2, SUB, half), BF16),
            pltpu.VMEM((2, 2, SUB, half), BF16),
            pltpu.VMEM((2, 2, SUB, half), BF16),
            pltpu.VMEM((2, chans, chans), BF16),
            pltpu.VMEM((rows - SUB, chans), BF16),
            pltpu.VMEM((rows - SUB, chans), BF16),
            pltpu.VMEM((rows - SUB, chans), BF16),
            dma((7,)),
            dma((per_line,)),
            dma((per_line,)),
            dma((lines,)),
            dma((lines,)),
            dma((per_line,)),
            dma((per_line,)),
            dma((2,)),
            dma((2,)),
            dma((2, 2)),
            dma((2, 2)),
            dma((4,)),
            dma((4,)),
            dma((4, 2)),
            dma((4, 2)),
            dma((4, 2)),
            dma((4, 2)),
            dma((4,)),
            dma((4,)),
            dma((steps,)),
            dma((steps,)),
            dma((steps,)),
            dma((steps,)),
        ],
        compiler_params=pltpu.CompilerParams(
            collective_id=0, has_side_effects=True, vmem_limit_bytes=56 * 1024 * 1024
        ),
    )(query, key_in, value, out_weight, rates.T, residues.T, skip_gain[None, :])


def solution(mesh):
    in_specs = (
        P("ctx", "tp"),
        P("ctx", "tp"),
        P("ctx", "tp"),
        P("tp", None),
        P("tp", None),
        P("tp"),
        P("tp", None),
    )
    lines = max(1, mesh.shape["ctx"] // MODES)
    return jax.shard_map(
        functools.partial(shards, lines),
        mesh=mesh,
        in_specs=in_specs,
        out_specs=P("ctx", "tp"),
        check_vma=False,
    )
```

```python
import functools

import jax
import jax.numpy as jnp
from jax import lax
from jax.experimental import pallas as pl
from jax.experimental.pallas import tpu as pltpu
from jax.sharding import PartitionSpec as P

GROUP = 16
MODES = 16
SUB = 128
LANES = 128
BLK = 256
STEP = 64
MESH = pl.DeviceIdType.MESH
F32 = jnp.float32
BF16 = jnp.bfloat16


def dot(a, b):
    return jnp.dot(a, b, preferred_element_type=F32)


def split(a):
    high = a.astype(BF16)
    return high, (a - high.astype(F32)).astype(BF16)


def kernel(
    lines,
    q_hbm,
    k_hbm,
    v_hbm,
    w_hbm,
    rates_ref,
    residues_ref,
    skip_ref,
    ob,
    qb,
    kb,
    vb,
    ub,
    wb,
    mixed,
    local,
    d_tab,
    a_hi,
    a_lo,
    h_pad,
    toep,
    sums,
    rate3,
    s_send,
    s_recv,
    l_send,
    l_recv,
    x_send,
    x_recv,
    far_s,
    far_r,
    near_s,
    near_r,
    wp,
    pair_r,
    sum_s,
    sum_r,
    lsem,
    s_ss,
    s_rs,
    l_ss,
    l_rs,
    x_ss,
    x_rs,
    far_ss,
    far_rs,
    near_ss,
    near_rs,
    wy_ss,
    wy_rs,
    wx_ss,
    wx_rs,
    wf_ss,
    wf_rs,
    sib_ss,
    sib_rs,
    pair_ss,
    pair_rs,
    sum_ss,
    sum_rs,
):
    rows, chans = ub.shape
    subs = rows // SUB
    groups = chans // GROUP
    blocks = chans // BLK
    half = chans // 2
    per_line = s_send.shape[0]
    own = s_send.shape[1]

    ctx, tp = lax.axis_index("ctx"), lax.axis_index("tp")
    mx, mj = lax.div(ctx, per_line), lax.rem(ctx, per_line)
    right, left = lax.rem(tp + 1, 4), lax.rem(tp + 3, 4)
    sides = ((ctx, right), (ctx, left))
    odd = lax.rem(tp, 2)
    pair, opp = tp + 1 - 2 * odd, 3 - tp
    way_pair, way_opp = odd, 1 - odd
    core = lax.rem(ctx, 2)
    sibling = ctx + 1 - 2 * core
    piece_rows = chans // 16
    pieces = 4
    step_rows = STEP
    steps = (rows - SUB) // step_rows

    order = sorted(range(1, per_line), key=lambda k: abs(2 * k - per_line))

    def peer_j(k):
        return lax.rem(mj + k, per_line)

    def peer_x(k):
        return lax.rem(mx + k, lines)

    barrier = pltpu.get_barrier_semaphore()
    for k in range(1, per_line):
        pl.semaphore_signal(
            barrier, inc=1, device_id=(mx * per_line + peer_j(k), tp), device_id_type=MESH
        )
    for k in range(1, lines):
        pl.semaphore_signal(
            barrier, inc=1, device_id=(peer_x(k) * per_line + mj, tp), device_id_type=MESH
        )
    for side in sides:
        pl.semaphore_signal(barrier, inc=1, device_id=side, device_id_type=MESH)

    loads = [
        pltpu.make_async_copy(k_hbm, kb, lsem.at[0]),
        pltpu.make_async_copy(v_hbm, vb, lsem.at[1]),
        pltpu.make_async_copy(q_hbm, qb, lsem.at[2]),
    ]
    w_loads = {}
    for r in (2, 1, 3, 0):
        start = pl.multiple_of(lax.rem(tp + r, 4) * chans, chans)
        w_loads[r] = pltpu.make_async_copy(
            w_hbm.at[:, pl.ds(start, chans)], wb.at[r], lsem.at[3 + r]
        )
    loads[0].start()
    loads[1].start()

    rates, residues = rates_ref[...].T, residues_ref[...].T
    pick = lax.broadcasted_iota(jnp.int32, (chans, MODES), 1) == (
        lax.broadcasted_iota(jnp.int32, (chans, MODES), 0) & (MODES - 1)
    )

    def column(a):
        spread = jnp.broadcast_to(a[:, None, :], (groups, MODES, MODES)).reshape(chans, MODES)
        return jnp.sum(jnp.where(pick, spread, 0.0), axis=1, keepdims=True)

    rate_col, residue_col = column(rates), column(residues)
    lag = lax.broadcasted_iota(jnp.int32, (chans, SUB), 1).astype(F32)
    decay_in = jnp.exp(-rate_col * (SUB - 1.0 - lag))
    high, low = split(decay_in)
    d_tab[:, :SUB] = high
    d_tab[:, SUB:] = low
    spread = (
        lax.shift_right_logical(lax.broadcasted_iota(jnp.int32, (groups, chans), 1), 4)
        == lax.broadcasted_iota(jnp.int32, (groups, chans), 0)
    ).astype(F32)
    rate_row = jnp.dot(
        rates_ref[...], spread, precision=lax.Precision.HIGHEST, preferred_element_type=F32
    )
    for k in range(chans // LANES):
        rate3[:, k, :] = rate_row[:, k * LANES : (k + 1) * LANES]
    same_group = lax.shift_right_logical(
        lax.broadcasted_iota(jnp.int32, (BLK, BLK), 0), 4
    ) == lax.shift_right_logical(lax.broadcasted_iota(jnp.int32, (BLK, BLK), 1), 4)
    diag = same_group.astype(F32)

    loads[0].wait()
    loads[1].wait()
    loads[2].start()
    for load in w_loads.values():
        load.start()
    for j in range(subs):
        at = pl.ds(j * SUB, SUB)
        for b in range(blocks):
            cols = pl.ds(b * BLK, BLK)
            u = (kb[at, cols].astype(F32) * vb[at, cols].astype(F32)).astype(BF16)
            ub[at, cols] = u
            full = dot(d_tab[cols, :], jnp.concatenate([u, u], axis=0))
            sums[j, :, cols] = jnp.sum((full * diag).reshape(BLK // MODES, MODES, BLK), axis=0)
    step_decay = jnp.exp(-rate_row * SUB)
    state = jnp.zeros_like(rate_row)
    for j in range(subs):
        following = step_decay * state + sums[j]
        sums[j] = state
        state = following
    for k in range(chans // LANES):
        piece = state[:, k * LANES : (k + 1) * LANES]
        s_send[:, :, k, :] = piece.reshape(per_line, own, LANES)

    pl.semaphore_wait(barrier, per_line - 1 + lines - 1 + 2)

    def s_copy(k):
        to = peer_j(k)
        return pltpu.make_async_remote_copy(
            src_ref=s_send.at[to],
            dst_ref=s_recv.at[mj],
            send_sem=s_ss.at[k],
            recv_sem=s_rs.at[k],
            device_id=(mx * per_line + to, tp),
            device_id_type=MESH,
        )

    def l_copy(k):
        return pltpu.make_async_remote_copy(
            src_ref=l_send,
            dst_ref=l_recv.at[mx],
            send_sem=l_ss.at[k],
            recv_sem=l_rs.at[k],
            device_id=(peer_x(k) * per_line + mj, tp),
            device_id_type=MESH,
        )

    def x_copy(k):
        to = peer_j(k)
        return pltpu.make_async_remote_copy(
            src_ref=x_send.at[to],
            dst_ref=x_recv.at[mj],
            send_sem=x_ss.at[k],
            recv_sem=x_rs.at[k],
            device_id=(mx * per_line + to, tp),
            device_id_type=MESH,
        )

    def piece(k, slot, lead, size):
        start = core * (chans // 2) + (k % 2) * (chans // 4) + slot * piece_rows + lead
        return pl.ds(pl.multiple_of(start, piece_rows // 2), size)

    def wy_copy(k):
        block = 1 - k // 2
        column = pair if block == 0 else 3 - pair
        at = piece(k, mx, 0, piece_rows)
        return pltpu.make_async_remote_copy(
            src_ref=w_hbm.at[at, pl.ds(pl.multiple_of(column * chans, chans), chans)],
            dst_ref=wp.at[block, at],
            send_sem=wy_ss.at[k],
            recv_sem=wy_rs.at[k],
            device_id=(ctx, pair),
            device_id_type=MESH,
        )

    def x_side(way):
        return (peer_x(1 if way == 0 else lines - 1) * per_line + mj, tp)

    def wx_copy(k, way):
        ref = wp.at[1 - k // 2, piece(k, mx, 0, piece_rows)]
        return pltpu.make_async_remote_copy(
            src_ref=ref,
            dst_ref=ref,
            send_sem=wx_ss.at[k, way],
            recv_sem=wx_rs.at[k, way],
            device_id=x_side(way),
            device_id_type=MESH,
        )

    def wf_copy(k, way):
        slot = peer_x(lines - 1 if way == 0 else 1)
        ref = wp.at[1 - k // 2, piece(k, slot, way * (piece_rows // 2), piece_rows // 2)]
        return pltpu.make_async_remote_copy(
            src_ref=ref,
            dst_ref=ref,
            send_sem=wf_ss.at[k, way],
            recv_sem=wf_rs.at[k, way],
            device_id=x_side(way),
            device_id_type=MESH,
        )

    def sib_copy(k):
        start = core * (chans // 2) + (k % 2) * (chans // 4)
        ref = wp.at[1 - k // 2, pl.ds(pl.multiple_of(start, chans // 4), chans // 4)]
        return pltpu.make_async_remote_copy(
            src_ref=ref,
            dst_ref=ref,
            send_sem=sib_ss.at[k],
            recv_sem=sib_rs.at[k],
            device_id=(sibling, tp),
            device_id_type=MESH,
        )

    def spread_piece(k):
        wy_copy(k).wait_recv()
        for way in range(2):
            wx_copy(k, way).start()

    def pass_piece(k):
        for way in range(2):
            wx_copy(k, way).wait_recv()
            wf_copy(k, way).start()

    def share_piece(k):
        for way in range(2):
            wf_copy(k, way).wait_recv()
        sib_copy(k).start()

    for k in order:
        s_copy(k).start()
    for k in range(pieces):
        wy_copy(k).start()
    s_recv[mj] = s_send[mj]

    taps = jnp.sum((decay_in * residue_col).reshape(groups, MODES, SUB), axis=1)
    h_pad[:, :SUB] = taps
    h_pad[:, SUB:] = jnp.zeros_like(taps)

    def build(n, carry):
        for side in range(2):
            row = jnp.broadcast_to(h_pad[pl.ds(2 * n + side, 1), :], (SUB, 2 * SUB))
            turned = pltpu.roll(row, SUB + 1, 1, stride=1, stride_axis=0)
            toep[n, :, side * SUB : (side + 1) * SUB] = turned[:, :SUB].astype(BF16)
        return carry

    lax.fori_loop(0, groups // 2, build, 0)

    my_rate = rate3[pl.ds(mj * own, own)]
    block_decay = jnp.exp(-my_rate * rows)
    weights = []
    for other in range(lines):
        distance = mx - 1 - other
        span = jnp.maximum(distance, 0) * (per_line * rows)
        weights.append(jnp.where(distance >= 0, jnp.exp(-my_rate * span.astype(F32)), 0.0))
    for k in range(1, per_line):
        s_copy(k).wait_recv()
    total = jnp.zeros_like(my_rate)
    for j in range(per_line):
        x_send[j] = total
        total = block_decay * total + s_recv[j]
    l_send[...] = total
    l_recv[mx] = total
    for k in range(1, lines):
        l_copy(k).start()
    spread_piece(0)

    def inside(n, carry):
        j, b = lax.div(n, blocks), lax.rem(n, blocks)
        at = pl.ds(pl.multiple_of(j * SUB, SUB), SUB)
        cols = pl.ds(pl.multiple_of(b * BLK, BLK), BLK)
        u = ub[at, cols]
        acc = skip_ref[:, cols] * u.astype(F32)
        lane_group = lax.shift_right_logical(lax.broadcasted_iota(jnp.int32, (1, BLK), 1), 4)
        for pair in range(BLK // GROUP // 2):
            masked = [
                u * (lane_group == 2 * pair + side).astype(F32).astype(BF16) for side in range(2)
            ]
            acc += dot(toep[b * (BLK // GROUP // 2) + pair], jnp.concatenate(masked, axis=0))
        local[at, cols] = acc
        return carry

    first_part = subs * blocks // 2
    lax.fori_loop(0, first_part, inside, 0)
    spread_piece(1)

    for k in range(1, lines):
        l_copy(k).wait_recv()
    entering = jnp.zeros_like(total)
    for other in range(lines):
        entering += weights[other] * l_recv[other]
    for j in range(per_line):
        x_send[j] = x_send[j] + entering
        entering = entering * block_decay
    for k in order:
        x_copy(k).start()
    x_recv[mj] = x_send[mj]

    high, low = split((residue_col * jnp.exp(-rate_col * (lag + 1.0))).T)
    a_hi[...] = high
    a_lo[...] = low
    lax.fori_loop(first_part, subs * blocks, inside, 0)
    pass_piece(0)
    spread_piece(2)
    pass_piece(1)
    loads[2].wait()
    for k in range(1, per_line):
        x_copy(k).wait_recv()

    def side_of(way):
        return (ctx, lax.rem(tp + 1 + 2 * way, 4))

    def far_copy(way):
        return pltpu.make_async_remote_copy(
            src_ref=far_s.at[way],
            dst_ref=far_r.at[way],
            send_sem=far_ss.at[way],
            recv_sem=far_rs.at[way],
            device_id=side_of(way),
            device_id_type=MESH,
        )

    def near_copy(way, part):
        return pltpu.make_async_remote_copy(
            src_ref=near_s.at[way, part],
            dst_ref=near_r.at[way, part],
            send_sem=near_ss.at[way, part],
            recv_sem=near_rs.at[way, part],
            device_id=side_of(way),
            device_id_type=MESH,
        )

    def tokens(h, skip=SUB, size=step_rows):
        return pl.ds(pl.multiple_of(skip + h * size, step_rows), size)

    def pair_copy(h):
        return pltpu.make_async_remote_copy(
            src_ref=mixed.at[tokens(h)],
            dst_ref=pair_r.at[tokens(h, 0)],
            send_sem=pair_ss.at[h],
            recv_sem=pair_rs.at[h],
            device_id=(ctx, pair),
            device_id_type=MESH,
        )

    def sum_copy(h):
        return pltpu.make_async_remote_copy(
            src_ref=sum_s.at[tokens(h, 0)],
            dst_ref=sum_r.at[tokens(h, 0)],
            send_sem=sum_ss.at[h],
            recv_sem=sum_rs.at[h],
            device_id=(ctx, opp),
            device_id_type=MESH,
        )

    def project(r, part):
        cols = pl.ds(pl.multiple_of(part * half, half), half)
        return dot(mixed[:SUB, :], wb[r, :, cols])

    w_loads[2].wait()
    entry = jnp.concatenate(
        [x_recv[:, :, k, :].reshape(MODES, LANES) for k in range(chans // LANES)], axis=1
    )
    diag_bf = diag.astype(BF16)

    def mix(j):
        at = pl.ds(pl.multiple_of(j * SUB, SUB), SUB)
        start = jnp.exp(-rate_row * (j * SUB * 1.0)) * entry + sums[j]
        x_hi, x_lo = split(start)
        for b in range(blocks):
            cols = slice(b * BLK, (b + 1) * BLK)
            wide_hi = jnp.concatenate([x_hi[:, cols]] * (BLK // MODES), axis=0) * diag_bf
            wide_lo = jnp.concatenate([x_lo[:, cols]] * (BLK // MODES), axis=0) * diag_bf
            past = dot(a_hi[:, cols], wide_hi) + dot(a_lo[:, cols], wide_hi)
            past += dot(a_hi[:, cols], wide_lo)
            mixed[at, cols] = (qb[at, cols].astype(F32) * (local[at, cols] + past)).astype(BF16)

    per_sub = SUB // step_rows

    def mix_and_send(j):
        mix(j)
        for h in range((j - 1) * per_sub, j * per_sub):
            pair_copy(h).start()

    def direct(way):
        near_s[way, 1 - way] = project(1 + 2 * way, 1 - way).astype(BF16)
        near_copy(way, 1 - way).start()

    def joint(way):
        part = project(1 + 2 * way, way)
        far_copy(way).wait_recv()
        near_s[way, way] = (part + far_r[way].astype(F32)).astype(BF16)
        near_copy(way, way).start()

    def far(way):
        far_s[way] = project(2, way).astype(BF16)
        far_copy(way).start()

    mix(0)
    far(way_pair)
    far(way_opp)
    mix_and_send(1)
    w_loads[1].wait()
    w_loads[3].wait()
    direct(way_opp)
    share_piece(0)
    for j in range(2, subs):
        mix_and_send(j)
    spread_piece(3)
    share_piece(1)
    joint(way_opp)
    direct(way_pair)
    joint(way_pair)
    pass_piece(2)
    w_loads[0].wait()
    for part in range(2):
        cols = slice(part * half, (part + 1) * half)
        local[:SUB, cols] = project(0, part)

    opp_slot = 3 - 2 * odd

    def sum_step(h):
        pair_copy(h).wait_recv()
        mine, theirs = mixed[tokens(h), :], pair_r[tokens(h, 0), :]
        for part in range(2):
            cols = slice(part * half, (part + 1) * half)
            both = dot(mine, wb[opp_slot, :, cols]) + dot(theirs, wp[1, :, cols])
            sum_s[tokens(h, 0), cols] = both.astype(BF16)
        sum_copy(h).start()

    def own_step(n):
        at, off = tokens(n, SUB, SUB), tokens(n, 0, SUB)
        mine, theirs = mixed[at, :], pair_r[off, :]
        for part in range(2):
            cols = slice(part * half, (part + 1) * half)
            local[at, cols] = dot(mine, wb[0, :, cols]) + dot(theirs, wp[0, :, cols])

    def finish(n):
        for h in range(n * per_sub, (n + 1) * per_sub):
            sum_copy(h).wait_recv()
            ob[tokens(h), :] = (local[tokens(h), :] + sum_r[tokens(h, 0), :].astype(F32)).astype(BF16)

    sib_copy(0).wait_recv()
    sib_copy(1).wait_recv()
    sum_step(0)
    pass_piece(3)
    share_piece(2)
    sum_step(1)
    share_piece(3)
    sum_step(2)
    sum_step(3)
    sib_copy(2).wait_recv()
    sib_copy(3).wait_recv()
    own_step(0)
    sum_step(4)
    sum_step(5)
    finish(0)
    own_step(1)
    own_step(2)
    finish(1)
    finish(2)
    for part in range(2):
        cols = slice(part * half, (part + 1) * half)
        near_copy(0, part).wait_recv()
        near_copy(1, part).wait_recv()
        total = local[:SUB, cols] + near_r[0, part].astype(F32) + near_r[1, part].astype(F32)
        ob[:SUB, cols] = total.astype(BF16)

    for way in range(2):
        far_copy(way).wait_send()
        for part in range(2):
            near_copy(way, part).wait_send()
        for k in range(pieces):
            wx_copy(k, way).wait_send()
            wf_copy(k, way).wait_send()
    for k in range(pieces):
        wy_copy(k).wait_send()
        sib_copy(k).wait_send()
    for h in range(steps):
        pair_copy(h).wait_send()
        sum_copy(h).wait_send()
    for k in range(1, per_line):
        s_copy(k).wait_send()
        x_copy(k).wait_send()
    for k in range(1, lines):
        l_copy(k).wait_send()


def shards(lines, query, key_in, value, rates, residues, skip_gain, out_weight):
    rows, chans = query.shape
    groups = chans // GROUP
    subs = rows // SUB
    steps = (rows - SUB) // STEP
    half = chans // 2
    per_line = lax.axis_size("ctx") // lines
    own = MODES // per_line
    tile = chans // LANES
    hbm = pl.BlockSpec(memory_space=pl.ANY)
    vmem = pl.BlockSpec(memory_space=pltpu.VMEM)
    dma = pltpu.SemaphoreType.DMA
    return pl.pallas_call(
        functools.partial(kernel, lines),
        name="hyena",
        out_shape=pltpu.VMEM((rows, chans), BF16),
        in_specs=[hbm, hbm, hbm, hbm, vmem, vmem, vmem],
        out_specs=vmem,
        scratch_shapes=[
            pltpu.VMEM((rows, chans), BF16),
            pltpu.VMEM((rows, chans), BF16),
            pltpu.VMEM((rows, chans), BF16),
            pltpu.VMEM((rows, chans), BF16),
            pltpu.VMEM((4, chans, chans), BF16),
            pltpu.VMEM((rows, chans), BF16),
            pltpu.VMEM((rows, chans), F32),
            pltpu.VMEM((chans, 2 * SUB), BF16),
            pltpu.VMEM((SUB, chans), BF16),
            pltpu.VMEM((SUB, chans), BF16),
            pltpu.VMEM((groups, 2 * SUB), F32),
            pltpu.VMEM((groups // 2, SUB, 2 * SUB), BF16),
            pltpu.VMEM((subs, MODES, chans), F32),
            pltpu.VMEM((MODES, tile, LANES), F32),
            pltpu.VMEM((per_line, own, tile, LANES), F32),
            pltpu.VMEM((per_line, own, tile, LANES), F32),
            pltpu.VMEM((own, tile, LANES), F32),
            pltpu.VMEM((lines, own, tile, LANES), F32),
            pltpu.VMEM((per_line, own, tile, LANES), F32),
            pltpu.VMEM((per_line, own, tile, LANES), F32),
            pltpu.VMEM((2, SUB, half), BF16),
            pltpu.VMEM((2, SUB, half), BF16),
            pltpu.VMEM((2, 2, SUB, half), BF16),
            pltpu.VMEM((2, 2, SUB, half), BF16),
            pltpu.VMEM((2, chans, chans), BF16),
            pltpu.VMEM((rows - SUB, chans), BF16),
            pltpu.VMEM((rows - SUB, chans), BF16),
            pltpu.VMEM((rows - SUB, chans), BF16),
            dma((7,)),
            dma((per_line,)),
            dma((per_line,)),
            dma((lines,)),
            dma((lines,)),
            dma((per_line,)),
            dma((per_line,)),
            dma((2,)),
            dma((2,)),
            dma((2, 2)),
            dma((2, 2)),
            dma((4,)),
            dma((4,)),
            dma((4, 2)),
            dma((4, 2)),
            dma((4, 2)),
            dma((4, 2)),
            dma((4,)),
            dma((4,)),
            dma((steps,)),
            dma((steps,)),
            dma((steps,)),
            dma((steps,)),
        ],
        compiler_params=pltpu.CompilerParams(
            collective_id=0, has_side_effects=True, vmem_limit_bytes=56 * 1024 * 1024
        ),
    )(query, key_in, value, out_weight, rates.T, residues.T, skip_gain[None, :])


def solution(mesh):
    in_specs = (
        P("ctx", "tp"),
        P("ctx", "tp"),
        P("ctx", "tp"),
        P("tp", None),
        P("tp", None),
        P("tp"),
        P("tp", None),
    )
    lines = max(1, mesh.shape["ctx"] // MODES)
    return jax.shard_map(
        functools.partial(shards, lines),
        mesh=mesh,
        in_specs=in_specs,
        out_specs=P("ctx", "tp"),
        check_vma=False,
    )
```
